32 devices in a mesh: member: 4 (over y, x), lat: 8 (over z, core).
Axes of the slice: x: 2, y: 2, z: 4, core: 2. Of those that a mesh axis runs over, the one named last changes fastest.
Arguments:
- initial_states: float32 [4, 16, 80, 128], P('member', 'lat'), may hold values from -6 to 6
- targets: float32 [2, 16, 80, 128], P(None, 'lat'), may hold values from -6 to 6
- lat_weight: float32 [16], P('lat'), may hold values from 0.3 to 3
- weight_in: float32 [256, 720], replicated, may hold values from -0.21875 to 0.21875
- weight_out: float32 [80, 2304], replicated, may hold values from -0.125 to 0.125
- hidden_bias: float32 [256], replicated, may hold values from -4 to 4
Outputs:
- state_grad: float32 [4, 16, 80, 128], P('member', 'lat')
- loss: float32 [], replicated
The draws below stay inside these ranges and needn't reach their ends.
All inputs are finite; a program needn't handle non-finite values.
Results may differ from the reference program's by a relative error of at most 0.00023.
Values sent between devices are 32-bit elements; how exact they have to be, the bound alone decides.
A program may use at most 64 MiB of HBM per device.

```python
import math
import jax
import jax.numpy as jnp
from jax import lax

VARS = 80
CH = 256
LON = 128
STEPS = 2
MEMBERS = 4
NLAT = 16


def shard_levels(stream_key, extent, pieces, low, high):
    level, own = 1.0, jax.random.fold_in(stream_key, 6)
    for axis_at, parts in pieces:
        steps = jnp.exp(jax.random.uniform(jax.random.fold_in(own, axis_at), (parts,), jnp.float32, low / len(pieces), high / len(pieces)))
        level = level * jnp.repeat(steps, extent[axis_at] // parts).reshape([-1 if axis == axis_at else 1 for axis in range(len(extent))])
    return level


def gaussian(stream_key, extent, width, bound, split=(), kind=jnp.bfloat16):
    loudness = shard_levels(stream_key, extent, split, -0.22, 0.18) if split else 1.0
    array = jax.random.normal(stream_key, extent, jnp.float32) * width * loudness
    return jnp.minimum(jnp.maximum(array, -bound), bound).astype(kind)


def setup_inputs(seed: int = 0) -> dict:
    key_of = jax.random.split(jax.random.key(seed), 7)
    initial_states = gaussian(key_of[0], (MEMBERS, NLAT, VARS, LON), 1.0, 6.0, ((0, 4), (1, 8)), jnp.float32)
    targets = gaussian(key_of[1], (STEPS, NLAT, VARS, LON), 1.0, 6.0, ((1, 8),), jnp.float32)
    lat_weight = jnp.clip(jnp.exp(math.log(3.0) - 2.3025851 * jax.random.uniform(key_of[2], (NLAT,), jnp.float32) ** shard_levels(key_of[2], (NLAT,), ((0, 8),), -0.2, 0.2)), 0.3, 3.0)
    weight_in = gaussian(key_of[3], (CH, 9 * VARS), (9 * VARS) ** -0.5, 0.21875, (), jnp.float32)
    weight_out = gaussian(key_of[4], (VARS, 9 * CH), (9 * CH) ** -0.5, 0.125, (), jnp.float32)
    hidden_bias = gaussian(key_of[5], (CH,), 1.0, 4.0, (), jnp.float32)
    return dict(initial_states=initial_states, targets=targets, lat_weight=lat_weight, weight_in=weight_in, weight_out=weight_out, hidden_bias=hidden_bias)


smooth_width = 0.1

def smooth(spread):
    return jnp.sqrt(spread * spread + smooth_width * smooth_width)

def convolve(field, matrix):
    height, channels, columns = field.shape
    padded = jnp.pad(field, ((1, 1), (0, 0), (1, 1)))
    blocks = matrix.reshape(matrix.shape[0], 9, channels)
    result = jnp.zeros((height, matrix.shape[0], columns), jnp.float32)
    for across in range(3):
        for along in range(3):
            result = result + jnp.einsum('oc,rcl->rol', blocks[:, 3 * across + along], padded[across:across + height, :, along:along + columns], precision=lax.Precision.HIGHEST)
    return result

def summed_loss(initial_states, targets, lat_weight, weight_in, weight_out, hidden_bias):

    def advance(member_field):
        before = convolve(member_field, weight_in) + hidden_bias[None, :, None]
        return member_field + convolve(jax.nn.gelu(before), weight_out)
    field = initial_states
    result = jnp.zeros((), jnp.float32)
    weights = lat_weight[:, None, None]
    for rollout in range(STEPS):
        field = lax.map(advance, field)
        direct = lax.optimization_barrier(jnp.sum(smooth(field - targets[rollout][None]), axis=0))

        def pair_row(single, field=field):
            return lax.optimization_barrier(jnp.sum(smooth(single[None] - field), axis=0))
        pairs = lax.optimization_barrier(jnp.sum(lax.map(pair_row, field), axis=0))
        result = result + jnp.sum(weights * (direct - pairs / (2.0 * (MEMBERS - 1))))
    return result

def reference(initial_states, targets, lat_weight, weight_in, weight_out, hidden_bias):
    result, gradient = jax.value_and_grad(summed_loss)(initial_states, targets, lat_weight, weight_in, weight_out, hidden_bias)
    loss = result / (MEMBERS * STEPS * NLAT * VARS * LON)
    return (gradient, loss)
```

```python
import functools

import jax
import jax.numpy as jnp
from jax import lax
from jax.experimental import pallas as pl
from jax.experimental.pallas import tpu as pltpu
from jax.sharding import PartitionSpec as P

smooth_width = 0.1
gelu_scale = 0.7978845608028654
gelu_cubic = 0.044715
MESH = pl.DeviceIdType.MESH
F32 = jnp.float32
BF16 = jnp.bfloat16


def split(value):
    high = value.astype(BF16)
    low = (value - high.astype(F32)).astype(BF16)
    return high, low


def shifted(value, tap):
    if tap == 1:
        return value
    columns = value.shape[-1]
    lane = lax.broadcasted_iota(jnp.int32, value.shape, 1)
    if tap == 0:
        return jnp.where(lane == 0, 0.0, pltpu.roll(value, 1, 1))
    return jnp.where(lane == columns - 1, 0.0, pltpu.roll(value, columns - 1, 1))


def dot(left, right):
    return jnp.dot(left, right, preferred_element_type=F32)


def kernel(
    members, bands,
    x_hbm, target_hbm, lat_hbm, w_in_hbm, w_out_hbm, bias_hbm,
    grad_ref, loss_ref,
    x_ref, target_ref, lat_ref, w_in_ref, w_out_ref, bias_ref, fetch_sem,
    halo, others, parts_m, parts_l, fields, grads, part_src,
    win, winb, wout, woutb, tall, s_high, s_low, h_high, h_low, before, slope, loss_grad, bias,
    halo_send, halo_recv, other_send, other_recv, pm_send, pm_recv, pl_send, pl_recv,
):
    steps, rows, chans, cols = target_ref.shape
    hidden = w_in_ref.shape[1]
    taps = 3 * chans
    depth = win.shape[2]
    deep = 3 * hidden
    me_m = lax.axis_index("member")
    me_l = lax.axis_index("lat")
    has_up = me_l > 0
    has_down = me_l < bands - 1

    fetches = [
        pltpu.make_async_copy(source, target, fetch_sem.at[n])
        for n, (source, target) in enumerate([
            (x_hbm, x_ref), (w_in_hbm, w_in_ref), (w_out_hbm, w_out_ref),
            (bias_hbm, bias_ref), (target_hbm, target_ref), (lat_hbm, lat_ref)])
    ]
    barrier = pltpu.get_barrier_semaphore()
    for k in range(1, members):
        pl.semaphore_signal(barrier, inc=1, device_id={"member": lax.rem(me_m + k, members)}, device_id_type=MESH)
    for k in range(1, bands):
        pl.semaphore_signal(barrier, inc=1, device_id={"lat": lax.rem(me_l + k, bands)}, device_id_type=MESH)

    for fetch in fetches:
        fetch.start()

    @pl.when(jnp.logical_not(has_up))
    def _():
        for n in range(2 * steps):
            halo[n, 0] = jnp.zeros(halo.shape[2:], F32)

    @pl.when(jnp.logical_not(has_down))
    def _():
        for n in range(2 * steps):
            halo[n, 1] = jnp.zeros(halo.shape[2:], F32)

    def to_up(n, source):
        return pltpu.make_async_remote_copy(
            src_ref=source.at[0:2], dst_ref=halo.at[n, 1],
            send_sem=halo_send.at[n, 0], recv_sem=halo_recv.at[n, 1],
            device_id={"lat": jnp.maximum(me_l - 1, 0)}, device_id_type=MESH)

    def to_down(n, source):
        return pltpu.make_async_remote_copy(
            src_ref=source.at[rows - 2:rows], dst_ref=halo.at[n, 0],
            send_sem=halo_send.at[n, 1], recv_sem=halo_recv.at[n, 0],
            device_id={"lat": jnp.minimum(me_l + 1, bands - 1)}, device_id_type=MESH)

    def halo_start(n, source):
        @pl.when(has_up)
        def _():
            to_up(n, source).start()

        @pl.when(has_down)
        def _():
            to_down(n, source).start()

    def halo_wait(n, source):
        @pl.when(has_up)
        def _():
            to_up(n, source).wait_send()
            to_down(n, source).wait_recv()

        @pl.when(has_down)
        def _():
            to_down(n, source).wait_send()
            to_up(n, source).wait_recv()

    def to_member(step, k):
        return pltpu.make_async_remote_copy(
            src_ref=fields.at[step], dst_ref=others.at[step, k - 1],
            send_sem=other_send.at[step, k - 1], recv_sem=other_recv.at[step, k - 1],
            device_id={"member": lax.rem(me_m + k, members)}, device_id_type=MESH)

    fetches[0].wait()
    pl.semaphore_wait(barrier, members + bands - 2)
    halo_start(0, x_ref)

    def put_wide(target, a, block):
        tall[0:taps, :] = block
        high, low = split(tall[...].T)
        target[a, 0:hidden] = high
        target[a, hidden:2 * hidden] = low

    def front_weights():
        for fetch in fetches[1:]:
            fetch.wait()
        tall[taps:, :] = jnp.zeros((depth - taps, hidden), F32)
        for a in range(3):
            put_wide(win, a, w_in_ref[a * taps:(a + 1) * taps, :])
        bias[...] = jnp.broadcast_to(bias_ref[...], (cols, hidden)).T
        for j in range(rows + 4):
            s_high[j * depth + taps:(j + 1) * depth, :] = jnp.zeros((depth - taps, cols), BF16)
            s_low[j * depth + taps:(j + 1) * depth, :] = jnp.zeros((depth - taps, cols), BF16)

    def narrow_weights():
        for a in range(3):
            for b in range(3):
                at = (3 * a + b) * hidden
                high, low = split(w_out_ref[:, at:at + hidden])
                wout[b * chans:(b + 1) * chans, a * hidden:(a + 1) * hidden] = high
                wout[taps + b * chans:taps + (b + 1) * chans, a * hidden:(a + 1) * hidden] = low

    def back_weights():
        for a in range(3):
            for b in range(3):
                at = (3 * (2 - a) + 2 - b) * chans
                high, low = split(w_in_ref[at:at + chans, :])
                winb[b * chans:(b + 1) * chans, a * hidden:(a + 1) * hidden] = high
                winb[taps + b * chans:taps + (b + 1) * chans, a * hidden:(a + 1) * hidden] = low
        for a in range(3):
            at = 3 * (2 - a) * hidden
            put_wide(woutb, a, jnp.concatenate(
                [w_out_ref[:, at + (2 - b) * hidden:at + (3 - b) * hidden] for b in range(3)], axis=0))

    def put_line(i, line):
        for b in range(3):
            high, low = split(shifted(line, b))
            at = i * depth + b * chans
            s_high[at:at + chans, :] = high
            s_low[at:at + chans, :] = low

    def widen_part(weights, inside):
        sums = {}
        for a in range(3):
            lines = [j for j in range(rows + 2) if (2 <= j + a < rows + 2) == inside]
            high = jnp.concatenate([s_high[(j + a) * depth:(j + a + 1) * depth, :] for j in lines], axis=1)
            low = jnp.concatenate([s_low[(j + a) * depth:(j + a + 1) * depth, :] for j in lines], axis=1)
            both = dot(weights[a], high)
            total = both[0:hidden] + both[hidden:2 * hidden] + dot(weights[a, 0:hidden, :], low)
            for n, j in enumerate(lines):
                line = total[:, n * cols:(n + 1) * cols]
                sums[j] = line if j not in sums else sums[j] + line
        return sums

    def widen_own(weights, own):
        for r in range(rows):
            put_line(r + 2, own[r])
        for j, line in widen_part(weights, True).items():
            before[:, j * cols:(j + 1) * cols] = line

    def widen_rest(weights, n):
        for j in range(2):
            put_line(j, halo[n, 0, j])
            put_line(rows + 2 + j, halo[n, 1, j])
        for j, line in widen_part(weights, False).items():
            before[:, j * cols:(j + 1) * cols] += line

    def narrow(weights):
        right = jnp.concatenate([h_high[r * hidden:r * hidden + deep, :] for r in range(rows)], axis=1)
        both = dot(weights[...], right)
        right = jnp.concatenate([h_low[r * hidden:r * hidden + deep, :] for r in range(rows)], axis=1)
        total = both[0:taps] + both[taps:2 * taps] + dot(weights[0:taps, :], right)
        result = []
        for r in range(rows):
            line = total[:, r * cols:(r + 1) * cols]
            result.append(sum(shifted(line[b * chans:(b + 1) * chans], b) for b in range(3)))
        return result

    def put_hidden(j, value):
        if j == 0:
            value = jnp.where(has_up, value, 0.0)
        if j == rows + 1:
            value = jnp.where(has_down, value, 0.0)
        high, low = split(value)
        h_high[j * hidden:(j + 1) * hidden, :] = high
        h_low[j * hidden:(j + 1) * hidden, :] = low

    def fold(value):
        return sum(value[8 * i:8 * i + 8] for i in range(chans // 8))

    def loss_terms(step):
        partial = jnp.zeros((8, cols), F32)
        for r in range(rows):
            weight = lat_ref[0:1, r:r + 1]
            mine = fields[step, r]
            error = mine - target_ref[step, r]
            square = error * error + smooth_width * smooth_width
            inverse = lax.rsqrt(square)
            direct = square * inverse
            gradient = error * inverse
            summed = jnp.full(mine.shape, smooth_width, F32)
            slopes = jnp.zeros_like(mine)
            for k in range(1, members):
                spread = mine - others[step, k - 1, r]
                square = spread * spread + smooth_width * smooth_width
                inverse = lax.rsqrt(square)
                summed = summed + square * inverse
                slopes = slopes + spread * inverse
            partial = partial + weight * fold(direct - summed / (2.0 * (members - 1)))
            loss_grad[step, r] = weight * (gradient - slopes / (members - 1))
        return partial

    for step in range(steps):
        own = x_ref if step == 0 else fields.at[step - 1]
        if step == 0:
            front_weights()
        widen_own(win, own)
        if step == 0:
            narrow_weights()
        halo_wait(step, own)
        widen_rest(win, step)
        for j in range(rows + 2):
            value = before[:, j * cols:(j + 1) * cols] + bias[...]
            inner = jnp.tanh(gelu_scale * (value + gelu_cubic * value * value * value))
            put_hidden(j, 0.5 * value * (1.0 + inner))
            slope[step, :, j * cols:(j + 1) * cols] = 0.5 * (1.0 + inner) + 0.5 * value * (1.0 - inner * inner) * (
                gelu_scale * (1.0 + 3.0 * gelu_cubic * value * value))
        change = narrow(wout)
        for r in range(rows):
            fields[step, r] = own[r] + change[r]
        if step < steps - 1:
            halo_start(step + 1, fields.at[step])
        for k in range(1, members):
            to_member(step, k).start()
        if step == 0:
            back_weights()

    partial = jnp.zeros((8, cols), F32)
    for step in range(steps):
        for k in range(1, members):
            to_member(step, k).wait()
        partial = partial + loss_terms(step)

    def part_to_member(k):
        return pltpu.make_async_remote_copy(
            src_ref=part_src.at[0], dst_ref=parts_m.at[me_m],
            send_sem=pm_send.at[k - 1], recv_sem=pm_recv.at[me_m],
            device_id={"member": lax.rem(me_m + k, members)}, device_id_type=MESH)

    def part_from_member(k):
        source = lax.rem(me_m + k, members)
        return pltpu.make_async_remote_copy(
            src_ref=part_src.at[0], dst_ref=parts_m.at[source],
            send_sem=pm_send.at[k - 1], recv_sem=pm_recv.at[source],
            device_id={"member": source}, device_id_type=MESH)

    def part_to_band(k):
        return pltpu.make_async_remote_copy(
            src_ref=part_src.at[1], dst_ref=parts_l.at[me_l],
            send_sem=pl_send.at[k - 1], recv_sem=pl_recv.at[me_l],
            device_id={"lat": lax.rem(me_l + k, bands)}, device_id_type=MESH)

    def part_from_band(k):
        source = lax.rem(me_l + k, bands)
        return pltpu.make_async_remote_copy(
            src_ref=part_src.at[1], dst_ref=parts_l.at[source],
            send_sem=pl_send.at[k - 1], recv_sem=pl_recv.at[source],
            device_id={"lat": source}, device_id_type=MESH)

    part_src[0] = partial

    for step in range(steps - 1, -1, -1):
        n = 2 * steps - 1 - step
        own = grads.at[step]
        for r in range(rows):
            if step == steps - 1:
                grads[step, r] = loss_grad[step, r]
            else:
                grads[step, r] = grads[step + 1, r] + change[r] + loss_grad[step, r]
        halo_start(n, own)
        if step == steps - 1:
            for k in range(1, members):
                part_to_member(k).start()
            parts_m[me_m] = partial
        else:
            if step == steps - 2:
                for k in range(1, members):
                    part_to_member(k).wait_send()
                    part_from_member(k).wait_recv()
                total = sum(parts_m[k] for k in range(members))
                part_src[1] = total
                for k in range(1, bands):
                    part_to_band(k).start()
                parts_l[me_l] = total
        widen_own(woutb, own)
        halo_wait(n, own)
        widen_rest(woutb, n)
        for j in range(rows + 2):
            put_hidden(j, before[:, j * cols:(j + 1) * cols] * slope[step, :, j * cols:(j + 1) * cols])
        change = narrow(winb)

    for r in range(rows):
        grad_ref[r] = grads[0, r] + change[r]
    for k in range(1, bands):
        part_to_band(k).wait_send()
        part_from_band(k).wait_recv()
    total = sum(parts_l[k] for k in range(bands))
    count = members * steps * rows * bands * chans * cols
    loss_ref[...] = jnp.full(loss_ref.shape, jnp.sum(total) / count, F32)


def deliver(grad_vmem, loss_vmem, grad_hbm, loss_hbm, loss_smem, sem):
    gradient = pltpu.make_async_copy(grad_vmem, grad_hbm, sem.at[0])
    loss = pltpu.make_async_copy(loss_smem, loss_hbm, sem.at[1])
    gradient.start()
    loss_smem[0, 0] = loss_vmem[0, 0]
    loss.start()
    loss.wait()
    gradient.wait()


def on_device(members, bands, initial_states, targets, lat_weight, weight_in, weight_out, hidden_bias):
    steps, rows, chans, cols = targets.shape
    hidden = weight_in.shape[0]
    taps = 3 * chans
    depth = -(-taps // 256) * 256
    deep = 3 * hidden
    vmem = pl.BlockSpec(memory_space=pltpu.VMEM)
    dma = pltpu.SemaphoreType.DMA
    gradient, loss = pl.pallas_call(
        functools.partial(kernel, members, bands),
        out_shape=(pltpu.VMEM((rows, chans, cols), F32), pltpu.VMEM((8, cols), F32)),
        in_specs=[pl.BlockSpec(memory_space=pltpu.HBM)] * 6,
        out_specs=(vmem, vmem),
        scratch_shapes=[
            pltpu.VMEM((rows, chans, cols), F32),
            pltpu.VMEM(targets.shape, F32),
            pltpu.VMEM((1, rows), F32),
            pltpu.VMEM((3 * taps, hidden), F32),
            pltpu.VMEM((chans, 3 * deep), F32),
            pltpu.VMEM((1, hidden), F32),
            dma((6,)),
            pltpu.VMEM((2 * steps, 2, 2, chans, cols), F32),
            pltpu.VMEM((steps, members - 1, rows, chans, cols), F32),
            pltpu.VMEM((members, 8, cols), F32),
            pltpu.VMEM((bands, 8, cols), F32),
            pltpu.VMEM((steps, rows, chans, cols), F32),
            pltpu.VMEM((steps, rows, chans, cols), F32),
            pltpu.VMEM((2, 8, cols), F32),
            pltpu.VMEM((3, 2 * hidden, depth), BF16),
            pltpu.VMEM((2 * taps, deep), BF16),
            pltpu.VMEM((2 * taps, deep), BF16),
            pltpu.VMEM((3, 2 * hidden, depth), BF16),
            pltpu.VMEM((depth, hidden), F32),
            pltpu.VMEM(((rows + 4) * depth, cols), BF16),
            pltpu.VMEM(((rows + 4) * depth, cols), BF16),
            pltpu.VMEM(((rows + 2) * hidden, cols), BF16),
            pltpu.VMEM(((rows + 2) * hidden, cols), BF16),
            pltpu.VMEM((hidden, (rows + 2) * cols), F32),
            pltpu.VMEM((steps, hidden, (rows + 2) * cols), F32),
            pltpu.VMEM((steps, rows, chans, cols), F32),
            pltpu.VMEM((hidden, cols), F32),
            dma((2 * steps, 2)), dma((2 * steps, 2)),
            dma((steps, members - 1)), dma((steps, members - 1)),
            dma((members - 1,)), dma((members,)),
            dma((bands - 1,)), dma((bands,)),
        ],
        compiler_params=pltpu.CompilerParams(collective_id=0, has_side_effects=True, vmem_limit_bytes=24 * 2**20),
    )(
        *(pltpu.with_memory_space_constraint(value, pltpu.HBM) for value in (
            initial_states.reshape(rows, chans, cols), targets, lat_weight.reshape(1, rows),
            weight_in.T, weight_out, hidden_bias.reshape(1, hidden)))
    )
    anywhere = pl.BlockSpec(memory_space=pl.ANY)
    gradient, loss = pl.pallas_call(
        deliver,
        out_shape=(jax.ShapeDtypeStruct((rows, chans, cols), F32), jax.ShapeDtypeStruct((1, 1), F32)),
        in_specs=[vmem, vmem],
        out_specs=(anywhere, anywhere),
        scratch_shapes=[pltpu.SMEM((1, 1), F32), dma((2,))],
    )(*(pltpu.with_memory_space_constraint(value, pltpu.VMEM) for value in (gradient, loss)))
    return gradient.reshape(initial_states.shape), loss.reshape(())


def solution(mesh):
    placed = (P("member", "lat", None, None), P(None, "lat", None, None), P("lat"), P(), P(), P())
    return jax.shard_map(
        functools.partial(on_device, mesh.shape["member"], mesh.shape["lat"]),
        mesh=mesh,
        in_specs=placed,
        out_specs=(P("member", "lat", None, None), P()),
        check_vma=False,
    )
```

```python
import functools

import jax
import jax.numpy as jnp
from jax import lax
from jax.experimental import pallas as pl
from jax.experimental.pallas import tpu as pltpu
from jax.sharding import PartitionSpec as P

smooth_width = 0.1
gelu_scale = 0.7978845608028654
gelu_cubic = 0.044715
MESH = pl.DeviceIdType.MESH
F32 = jnp.float32
BF16 = jnp.bfloat16


def split(value):
    high = value.astype(BF16)
    low = (value - high.astype(F32)).astype(BF16)
    return high, low


def shifted(value, tap):
    if tap == 1:
        return value
    columns = value.shape[-1]
    lane = lax.broadcasted_iota(jnp.int32, value.shape, 1)
    if tap == 0:
        return jnp.where(lane == 0, 0.0, pltpu.roll(value, 1, 1))
    return jnp.where(lane == columns - 1, 0.0, pltpu.roll(value, columns - 1, 1))


def dot(left, right):
    return jnp.dot(left, right, preferred_element_type=F32)


def kernel(
    members, bands,
    x_hbm, target_hbm, lat_hbm, w_in_hbm, w_out_hbm, bias_hbm,
    grad_ref, loss_ref,
    x_ref, target_ref, lat_ref, w_in_ref, w_out_ref, bias_ref, fetch_sem,
    halo, others, parts_m, parts_l, fields, grads, part_src,
    win, winb, wout, woutb, tall, s_high, s_low, h_high, h_low, before, slope, narrowed, loss_grad, bias,
    halo_send, halo_recv, other_send, other_recv, pm_send, pm_recv, pl_send, pl_recv,
):
    steps, rows, chans, cols = target_ref.shape
    hidden = w_in_ref.shape[1]
    taps = 3 * chans
    depth = win.shape[2]
    me_m = lax.axis_index("member")
    me_l = lax.axis_index("lat")
    odd = lax.rem(me_l, 2)
    slow = me_l - 1 + 2 * odd
    fast = me_l + 1 - 2 * odd
    has_slow = jnp.logical_and(slow >= 0, slow < bands)
    slow = jnp.clip(slow, 0, bands - 1)

    def mirrored(n, last):
        return n + odd * (last - 2 * n)

    fetches = [
        pltpu.make_async_copy(source, target, fetch_sem.at[n])
        for n, (source, target) in enumerate(
            [(x_hbm.at[mirrored(i, rows - 1)], x_ref.at[i]) for i in range(rows)]
            + [(w_in_hbm, w_in_ref), (w_out_hbm, w_out_ref), (bias_hbm, bias_ref), (lat_hbm, lat_ref)]
            + [(target_hbm.at[:, mirrored(i, rows - 1)], target_ref.at[:, i]) for i in range(rows)])
    ]
    barrier = pltpu.get_barrier_semaphore()
    for k in range(1, members):
        pl.semaphore_signal(barrier, inc=1, device_id={"member": lax.rem(me_m + k, members)}, device_id_type=MESH)
    for k in range(1, bands):
        pl.semaphore_signal(barrier, inc=1, device_id={"lat": lax.rem(me_l + k, bands)}, device_id_type=MESH)

    for fetch in fetches:
        fetch.start()

    @pl.when(jnp.logical_not(has_slow))
    def _():
        for n in range(2 * steps):
            halo[n, 0] = jnp.zeros(halo.shape[2:], F32)

    def to_slow(n, source, far):
        return pltpu.make_async_remote_copy(
            src_ref=source.at[far], dst_ref=halo.at[n, 0, far],
            send_sem=halo_send.at[n, 0, far], recv_sem=halo_recv.at[n, 0, far],
            device_id={"lat": slow}, device_id_type=MESH)

    def to_fast(n, source, far):
        return pltpu.make_async_remote_copy(
            src_ref=source.at[rows - 1 - far], dst_ref=halo.at[n, 1, far],
            send_sem=halo_send.at[n, 1, far], recv_sem=halo_recv.at[n, 1, far],
            device_id={"lat": fast}, device_id_type=MESH)

    def slow_start(n, source, fars=(0, 1)):
        @pl.when(has_slow)
        def _():
            for far in fars:
                to_slow(n, source, far).start()

    def slow_wait(n, source, far):
        @pl.when(has_slow)
        def _():
            to_slow(n, source, far).wait_recv()

    def halo_start(n, source):
        slow_start(n, source)
        for far in range(2):
            to_fast(n, source, far).start()

    def peer(k):
        if members & (members - 1):
            return lax.rem(me_m + k, members)
        result, bit = 0, 1
        while bit < members:
            mine = lax.rem(me_m // bit, 2)
            result = result + bit * (1 - mine if k & bit else mine)
            bit *= 2
        return result

    peers = sorted(range(1, members), key=lambda k: -bin(k).count("1"))

    def to_member(step, k, i):
        return pltpu.make_async_remote_copy(
            src_ref=fields.at[step, i], dst_ref=others.at[step, k - 1, i],
            send_sem=other_send.at[step, k - 1, i], recv_sem=other_recv.at[step, k - 1, i],
            device_id={"member": peer(k)}, device_id_type=MESH)

    for fetch in fetches[:rows]:
        fetch.wait()
    pl.semaphore_wait(barrier, members + bands - 2)
    halo_start(0, x_ref)

    def put_wide(target, a, block):
        tall[0:taps, :] = block
        high, low = split(tall[...].T)
        target[a, 0:hidden] = high
        target[a, hidden:2 * hidden] = low

    def tap_rows(a):
        return pl.ds(pl.multiple_of(mirrored(a, 2) * taps, 8), taps)

    def tap_block(a, b, size, unit):
        return pl.ds(pl.multiple_of((3 * mirrored(a, 2) + b) * size, unit), size)

    def front_weights():
        fetches[rows].wait()
        fetches[rows + 2].wait()
        tall[taps:, :] = jnp.zeros((depth - taps, hidden), F32)
        for a in range(3):
            put_wide(win, a, w_in_ref[tap_rows(a), :])
        bias[...] = jnp.broadcast_to(bias_ref[...], (cols, hidden)).T
        for t in range(rows + 4):
            s_high[t * depth + taps:(t + 1) * depth, :] = jnp.zeros((depth - taps, cols), BF16)
            s_low[t * depth + taps:(t + 1) * depth, :] = jnp.zeros((depth - taps, cols), BF16)

    def narrow_weights():
        fetches[rows + 1].wait()
        for a in range(3):
            for b in range(3):
                high, low = split(w_out_ref[:, tap_block(a, b, hidden, 128)])
                wout[b * chans:(b + 1) * chans, a * hidden:(a + 1) * hidden] = high
                wout[taps + b * chans:taps + (b + 1) * chans, a * hidden:(a + 1) * hidden] = low

    def back_weights():
        for a in range(3):
            for b in range(3):
                high, low = split(w_in_ref[tap_block(2 - a, 2 - b, chans, 8), :])
                winb[b * chans:(b + 1) * chans, a * hidden:(a + 1) * hidden] = high
                winb[taps + b * chans:taps + (b + 1) * chans, a * hidden:(a + 1) * hidden] = low
        for a in range(3):
            put_wide(woutb, a, jnp.concatenate(
                [w_out_ref[:, tap_block(2 - a, 2 - b, hidden, 128)] for b in range(3)], axis=0))

    def put_line(t, line):
        for b in range(3):
            high, low = split(shifted(line, b))
            at = t * depth + b * chans
            s_high[at:at + chans, :] = high
            s_low[at:at + chans, :] = low

    def joined(ref, size, lines):
        return jnp.concatenate([ref[t * size:(t + 1) * size, :] for t in lines], axis=1)

    def widen(weights, parts):
        sums = {}
        for a, lines in parts:
            high = joined(s_high, depth, lines)
            low = joined(s_low, depth, lines)
            both = dot(weights[a], high)
            total = both[0:hidden] + both[hidden:2 * hidden] + dot(weights[a, 0:hidden, :], low)
            for n, t in enumerate(lines):
                line = total[:, n * cols:(n + 1) * cols]
                sums[t - a] = line if t - a not in sums else sums[t - a] + line
        return sums

    def narrow(weights, parts):
        sums = {}
        for a, outs in parts:
            lines = [i + a for i in outs]
            at = a * hidden
            both = dot(weights[:, at:at + hidden], joined(h_high, hidden, lines))
            total = both[0:taps] + both[taps:2 * taps] + dot(
                weights[0:taps, at:at + hidden], joined(h_low, hidden, lines))
            for n, i in enumerate(outs):
                line = total[:, n * cols:(n + 1) * cols]
                sums[i] = line if i not in sums else sums[i] + line
        return sums

    def put_hidden(j, value):
        if j == 0:
            value = jnp.where(has_slow, value, 0.0)
        high, low = split(value)
        h_high[j * hidden:(j + 1) * hidden, :] = high
        h_low[j * hidden:(j + 1) * hidden, :] = low

    def bend(step, j, value):
        value = value + bias[...]
        inner = jnp.tanh(gelu_scale * (value + gelu_cubic * value * value * value))
        put_hidden(j, 0.5 * value * (1.0 + inner))
        slope[step, j] = 0.5 * (1.0 + inner) + 0.5 * value * (1.0 - inner * inner) * (
            gelu_scale * (1.0 + 3.0 * gelu_cubic * value * value))

    def unbend(step, j, value):
        put_hidden(j, value * slope[step, j])

    def own_part(weights, own):
        for i in range(rows):
            put_line(i + 2, own[i])
        for j, line in widen(weights, [(a, range(2, rows + 2)) for a in range(3)]).items():
            before[j] = line

    def convolve(wide, slim, n, own, act):
        for far in range(2):
            to_fast(n, own, far).wait_recv()
            put_line(rows + 2 + far, halo[n, 1, far])
        sums = widen(wide, [(2, (rows + 2, rows + 3)), (1, (rows + 2,))])
        for j in range(2, rows + 2):
            act(j, before[j] + sums[j] if j in sums else before[j])
        early = [(a, [i for i in range(rows) if i + a >= 2]) for a in (2, 1, 0)]
        for i, line in narrow(slim, [part for part in early if part[1]]).items():
            narrowed[i] = line
        slow_wait(n, own, 0)
        put_line(1, halo[n, 0, 0])
        sums = widen(wide, [(0, (1,)), (1, (1,))])
        before[0] += sums[0]
        act(1, before[1] + sums[1])
        slow_wait(n, own, 1)
        put_line(0, halo[n, 0, 1])
        act(0, before[0] + widen(wide, [(0, (0,))])[0])
        sums = narrow(slim, [(1, (0,)), (0, (0, 1))])
        result = []
        for i in range(rows):
            line = narrowed[i] + sums[i] if i in sums else narrowed[i]
            result.append(sum(shifted(line[b * chans:(b + 1) * chans], b) for b in range(3)))
        return result

    def fold(value):
        return sum(value[8 * i:8 * i + 8] for i in range(chans // 8))

    def loss_terms(step, i):
        weight = jnp.where(odd == 1, lat_ref[0:1, rows - 1 - i:rows - i], lat_ref[0:1, i:i + 1])
        mine = fields[step, i]
        error = mine - target_ref[step, i]
        square = error * error + smooth_width * smooth_width
        inverse = lax.rsqrt(square)
        direct = square * inverse
        gradient = error * inverse
        summed = jnp.full(mine.shape, smooth_width, F32)
        slopes = jnp.zeros_like(mine)
        for k in range(1, members):
            spread = mine - others[step, k - 1, i]
            square = spread * spread + smooth_width * smooth_width
            inverse = lax.rsqrt(square)
            summed = summed + square * inverse
            slopes = slopes + spread * inverse
        loss_grad[step, i] = weight * (gradient - slopes / (members - 1))
        return weight * fold(direct - summed / (2.0 * (members - 1)))

    for step in range(steps):
        own = x_ref if step == 0 else fields.at[step - 1]
        if step == 0:
            front_weights()
        own_part(win, own)
        if step == 0:
            narrow_weights()
        else:
            back_weights()
        change = convolve(win, wout, step, own, functools.partial(bend, step))
        for i in range(rows):
            fields[step, i] = own[i] + change[i]
        if step < steps - 1:
            halo_start(step + 1, fields.at[step])
        for i in range(rows):
            for k in peers:
                to_member(step, k, i).start()

    for fetch in fetches[rows + 3:]:
        fetch.wait()
    partial = jnp.zeros((8, cols), F32)
    for step in range(steps):
        for i in range(rows):
            for k in peers:
                to_member(step, k, i).wait()
            partial = partial + loss_terms(step, i)
            if step == steps - 1:
                grads[step, i] = loss_grad[step, i]
                if i < 2:
                    slow_start(steps, grads.at[step], (i,))
                if rows - 1 - i < 2:
                    to_fast(steps, grads.at[step], rows - 1 - i).start()

    def part_to_member(k):
        return pltpu.make_async_remote_copy(
            src_ref=part_src.at[0], dst_ref=parts_m.at[me_m],
            send_sem=pm_send.at[k - 1], recv_sem=pm_recv.at[me_m],
            device_id={"member": lax.rem(me_m + k, members)}, device_id_type=MESH)

    def part_from_member(k):
        source = lax.rem(me_m + k, members)
        return pltpu.make_async_remote_copy(
            src_ref=part_src.at[0], dst_ref=parts_m.at[source],
            send_sem=pm_send.at[k - 1], recv_sem=pm_recv.at[source],
            device_id={"member": source}, device_id_type=MESH)

    def part_to_band(k):
        return pltpu.make_async_remote_copy(
            src_ref=part_src.at[1], dst_ref=parts_l.at[me_l],
            send_sem=pl_send.at[k - 1], recv_sem=pl_recv.at[me_l],
            device_id={"lat": lax.rem(me_l + k, bands)}, device_id_type=MESH)

    def part_from_band(k):
        source = lax.rem(me_l + k, bands)
        return pltpu.make_async_remote_copy(
            src_ref=part_src.at[1], dst_ref=parts_l.at[source],
            send_sem=pl_send.at[k - 1], recv_sem=pl_recv.at[source],
            device_id={"lat": source}, device_id_type=MESH)

    part_src[0] = partial

    for step in range(steps - 1, -1, -1):
        n = 2 * steps - 1 - step
        own = grads.at[step]
        if step == steps - 1:
            for k in range(1, members):
                part_to_member(k).start()
            parts_m[me_m] = partial
        else:
            for i in range(rows):
                grads[step, i] = grads[step + 1, i] + change[i] + loss_grad[step, i]
            halo_start(n, own)
            if step == steps - 2:
                for k in range(1, members):
                    part_to_member(k).wait_send()
                    part_from_member(k).wait_recv()
                total = sum(parts_m[k] for k in range(members))
                part_src[1] = total
                for k in range(1, bands):
                    part_to_band(k).start()
                parts_l[me_l] = total
        own_part(woutb, own)
        change = convolve(woutb, winb, n, own, functools.partial(unbend, step))

    for i in range(rows):
        grad_ref[mirrored(i, rows - 1)] = grads[0, i] + change[i]
    for k in range(1, bands):
        part_to_band(k).wait_send()
        part_from_band(k).wait_recv()
    total = sum(parts_l[k] for k in range(bands))
    count = members * steps * rows * bands * chans * cols
    loss_ref[...] = jnp.full(loss_ref.shape, jnp.sum(total) / count, F32)
    for n in range(2 * steps):
        own = x_ref if n == 0 else fields.at[n - 1] if n < steps else grads.at[2 * steps - 1 - n]
        for far in range(2):
            to_fast(n, own, far).wait_send()

        @pl.when(has_slow)
        def _():
            for far in range(2):
                to_slow(n, own, far).wait_send()


def deliver(grad_vmem, loss_vmem, grad_hbm, loss_hbm, loss_smem, sem):
    gradient = pltpu.make_async_copy(grad_vmem, grad_hbm, sem.at[0])
    loss = pltpu.make_async_copy(loss_smem, loss_hbm, sem.at[1])
    gradient.start()
    loss_smem[0, 0] = loss_vmem[0, 0]
    loss.start()
    loss.wait()
    gradient.wait()


def on_device(members, bands, initial_states, targets, lat_weight, weight_in, weight_out, hidden_bias):
    steps, rows, chans, cols = targets.shape
    hidden = weight_in.shape[0]
    taps = 3 * chans
    depth = -(-taps // 256) * 256
    deep = 3 * hidden
    vmem = pl.BlockSpec(memory_space=pltpu.VMEM)
    dma = pltpu.SemaphoreType.DMA
    gradient, loss = pl.pallas_call(
        functools.partial(kernel, members, bands),
        out_shape=(pltpu.VMEM((rows, chans, cols), F32), pltpu.VMEM((8, cols), F32)),
        in_specs=[pl.BlockSpec(memory_space=pltpu.HBM)] * 6,
        out_specs=(vmem, vmem),
        scratch_shapes=[
            pltpu.VMEM((rows, chans, cols), F32),
            pltpu.VMEM(targets.shape, F32),
            pltpu.VMEM((1, rows), F32),
            pltpu.VMEM((3 * taps, hidden), F32),
            pltpu.VMEM((chans, 3 * deep), F32),
            pltpu.VMEM((1, hidden), F32),
            dma((2 * rows + 4,)),
            pltpu.VMEM((2 * steps, 2, 2, chans, cols), F32),
            pltpu.VMEM((steps, members - 1, rows, chans, cols), F32),
            pltpu.VMEM((members, 8, cols), F32),
            pltpu.VMEM((bands, 8, cols), F32),
            pltpu.VMEM((steps, rows, chans, cols), F32),
            pltpu.VMEM((steps, rows, chans, cols), F32),
            pltpu.VMEM((2, 8, cols), F32),
            pltpu.VMEM((3, 2 * hidden, depth), BF16),
            pltpu.VMEM((2 * taps, deep), BF16),
            pltpu.VMEM((2 * taps, deep), BF16),
            pltpu.VMEM((3, 2 * hidden, depth), BF16),
            pltpu.VMEM((depth, hidden), F32),
            pltpu.VMEM(((rows + 4) * depth, cols), BF16),
            pltpu.VMEM(((rows + 4) * depth, cols), BF16),
            pltpu.VMEM(((rows + 2) * hidden, cols), BF16),
            pltpu.VMEM(((rows + 2) * hidden, cols), BF16),
            pltpu.VMEM((rows + 2, hidden, cols), F32),
            pltpu.VMEM((steps, rows + 2, hidden, cols), F32),
            pltpu.VMEM((rows, taps, cols), F32),
            pltpu.VMEM((steps, rows, chans, cols), F32),
            pltpu.VMEM((hidden, cols), F32),
            dma((2 * steps, 2, 2)), dma((2 * steps, 2, 2)),
            dma((steps, members - 1, rows)), dma((steps, members - 1, rows)),
            dma((members - 1,)), dma((members,)),
            dma((bands - 1,)), dma((bands,)),
        ],
        compiler_params=pltpu.CompilerParams(collective_id=0, has_side_effects=True, vmem_limit_bytes=24 * 2**20),
    )(
        *(pltpu.with_memory_space_constraint(value, pltpu.HBM) for value in (
            initial_states.reshape(rows, chans, cols), targets, lat_weight.reshape(1, rows),
            weight_in.T, weight_out, hidden_bias.reshape(1, hidden)))
    )
    anywhere = pl.BlockSpec(memory_space=pl.ANY)
    gradient, loss = pl.pallas_call(
        deliver,
        out_shape=(jax.ShapeDtypeStruct((rows, chans, cols), F32), jax.ShapeDtypeStruct((1, 1), F32)),
        in_specs=[vmem, vmem],
        out_specs=(anywhere, anywhere),
        scratch_shapes=[pltpu.SMEM((1, 1), F32), dma((2,))],
    )(*(pltpu.with_memory_space_constraint(value, pltpu.VMEM) for value in (gradient, loss)))
    return gradient.reshape(initial_states.shape), loss.reshape(())


def solution(mesh):
    placed = (P("member", "lat", None, None), P(None, "lat", None, None), P("lat"), P(), P(), P())
    return jax.shard_map(
        functools.partial(on_device, mesh.shape["member"], mesh.shape["lat"]),
        mesh=mesh,
        in_specs=placed,
        out_specs=(P("member", "lat", None, None), P()),
        check_vma=False,
    )
```

```python
import functools

import jax
import jax.numpy as jnp
from jax import lax
from jax.experimental import pallas as pl
from jax.experimental.pallas import tpu as pltpu
from jax.sharding import PartitionSpec as P

smooth_width = 0.1
gelu_scale = 0.7978845608028654
gelu_cubic = 0.044715
MESH = pl.DeviceIdType.MESH
F32 = jnp.float32
BF16 = jnp.bfloat16


def split(value):
    high = value.astype(BF16)
    low = (value - high.astype(F32)).astype(BF16)
    return high, low


def shifted(value, tap):
    if tap == 1:
        return value
    columns = value.shape[-1]
    lane = lax.broadcasted_iota(jnp.int32, value.shape, 1)
    if tap == 0:
        return jnp.where(lane == 0, 0.0, pltpu.roll(value, 1, 1))
    return jnp.where(lane == columns - 1, 0.0, pltpu.roll(value, columns - 1, 1))


def dot(left, right):
    return jnp.dot(left, right, preferred_element_type=F32)


def kernel(
    members, bands,
    x_hbm, target_hbm, lat_hbm, w_in_hbm, w_out_hbm, bias_hbm,
    grad_ref, loss_ref,
    x_ref, target_ref, lat_ref, w_in_ref, w_out_ref, bias_ref, fetch_sem,
    halo, others, parts, fields, grads,
    win, winb, wout, woutb, tall, s_high, s_low, h_high, h_low, before, slope, narrowed, loss_grad, bias,
    halo_send, slow_recv, fast_recv, other_send, other_recv, part_send, part_recv, reach,
):
    steps, rows, chans, cols = target_ref.shape
    hidden = w_in_ref.shape[1]
    taps = 3 * chans
    depth = win.shape[2]
    me_m = lax.axis_index("member")
    me_l = lax.axis_index("lat")
    odd = lax.rem(me_l, 2)
    slow = me_l - 1 + 2 * odd
    fast = me_l + 1 - 2 * odd
    has_slow = jnp.logical_and(slow >= 0, slow < bands)
    slow = jnp.clip(slow, 0, bands - 1)

    def mirrored(n, last):
        return n + odd * (last - 2 * n)

    def fetch(n, copies):
        return [pltpu.make_async_copy(source, target, fetch_sem.at[n]) for source, target in copies]

    mirror = [mirrored(i, rows - 1) for i in range(rows)]
    fetches = [
        fetch(0, [(x_hbm.at[mirror[i]], x_ref.at[i]) for i in range(rows)]),
        fetch(1, [(w_in_hbm, w_in_ref)]),
        fetch(2, [(bias_hbm, bias_ref)]),
        fetch(3, [(w_out_hbm, w_out_ref)]),
        fetch(4, [(target_hbm.at[:, mirror[i]], target_ref.at[:, i]) for i in range(rows)]),
        fetch(5, [(lat_hbm, lat_ref)]),
    ]
    arrivals = [x_ref, w_in_ref, bias_ref, w_out_ref, target_ref, lat_ref]

    def arrive(n):
        pltpu.make_async_copy(arrivals[n], arrivals[n], fetch_sem.at[n]).wait()

    for copy in fetches[0]:
        copy.start()
    barrier = pltpu.get_barrier_semaphore()
    for k in range(1, members):
        pl.semaphore_signal(barrier, inc=1, device_id={"member": lax.rem(me_m + k, members)}, device_id_type=MESH)
    pl.semaphore_signal(barrier, inc=1, device_id={"lat": fast}, device_id_type=MESH)

    @pl.when(has_slow)
    def _():
        pl.semaphore_signal(barrier, inc=1, device_id={"lat": slow}, device_id_type=MESH)

    for copies in fetches[1:]:
        for copy in copies:
            copy.start()

    @pl.when(jnp.logical_not(has_slow))
    def _():
        for n in range(2 * steps):
            halo[n, 0] = jnp.zeros(halo.shape[2:], F32)

    def to_slow(n, source, far):
        return pltpu.make_async_remote_copy(
            src_ref=source.at[far], dst_ref=halo.at[n, 0, far],
            send_sem=halo_send.at[0], recv_sem=slow_recv.at[n, far],
            device_id={"lat": slow}, device_id_type=MESH)

    def to_fast(n, source, far):
        return pltpu.make_async_remote_copy(
            src_ref=source.at[rows - 1 - far], dst_ref=halo.at[n, 1, far],
            send_sem=halo_send.at[1], recv_sem=fast_recv.at[n],
            device_id={"lat": fast}, device_id_type=MESH)

    def slow_start(n, source, fars=(0, 1)):
        @pl.when(has_slow)
        def _():
            for far in fars:
                to_slow(n, source, far).start()

    def slow_wait(n, source, far):
        @pl.when(has_slow)
        def _():
            to_slow(n, source, far).wait_recv()

    def halo_start(n, source):
        slow_start(n, source)
        for far in range(2):
            to_fast(n, source, far).start()

    def peer(k):
        if members & (members - 1):
            return lax.rem(me_m + k, members)
        result, bit = 0, 1
        while bit < members:
            mine = lax.rem(me_m // bit, 2)
            result = result + bit * (1 - mine if k & bit else mine)
            bit *= 2
        return result

    peers = sorted(range(1, members), key=lambda k: -bin(k).count("1"))

    def to_member(step, k, i):
        return pltpu.make_async_remote_copy(
            src_ref=fields.at[step, i], dst_ref=others.at[step, k - 1, i],
            send_sem=other_send.at[0], recv_sem=other_recv.at[step, i],
            device_id={"member": peer(k)}, device_id_type=MESH)

    rounds = [1]
    while 2 * rounds[-1] < bands - 1:
        rounds.append(2 * rounds[-1])

    def reach_out(r):
        for far in (me_l - rounds[r], me_l + rounds[r]):
            @pl.when(jnp.logical_and(far >= 0, far < bands))
            def _():
                pl.semaphore_signal(
                    reach.at[r], inc=1, device_id={"lat": jnp.clip(far, 0, bands - 1)}, device_id_type=MESH)

    def reached(r):
        below = (me_l >= rounds[r]).astype(jnp.int32)
        above = (me_l + rounds[r] < bands).astype(jnp.int32)
        pl.semaphore_wait(reach.at[r], below + above)

    arrive(0)
    pl.semaphore_wait(barrier, members + has_slow.astype(jnp.int32))
    halo_start(0, x_ref)
    reach_out(0)

    def put_wide(target, a, block):
        tall[0:taps, :] = block
        high, low = split(tall[...].T)
        target[a, 0:hidden] = high
        target[a, hidden:2 * hidden] = low

    def tap_rows(a):
        return pl.ds(pl.multiple_of(mirrored(a, 2) * taps, 8), taps)

    def tap_block(a, b, size, unit):
        return pl.ds(pl.multiple_of((3 * mirrored(a, 2) + b) * size, unit), size)

    def front_weights():
        arrive(1)
        arrive(2)
        tall[taps:, :] = jnp.zeros((depth - taps, hidden), F32)
        for a in range(3):
            put_wide(win, a, w_in_ref[tap_rows(a), :])
        bias[...] = jnp.broadcast_to(bias_ref[...], (cols, hidden)).T
        for t in range(rows + 4):
            s_high[t * depth + taps:(t + 1) * depth, :] = jnp.zeros((depth - taps, cols), BF16)
            s_low[t * depth + taps:(t + 1) * depth, :] = jnp.zeros((depth - taps, cols), BF16)

    def narrow_weights():
        arrive(3)
        for a in range(3):
            for b in range(3):
                high, low = split(w_out_ref[:, tap_block(a, b, hidden, 128)])
                wout[b * chans:(b + 1) * chans, a * hidden:(a + 1) * hidden] = high
                wout[taps + b * chans:taps + (b + 1) * chans, a * hidden:(a + 1) * hidden] = low

    def back_weights():
        for a in range(3):
            for b in range(3):
                high, low = split(w_in_ref[tap_block(2 - a, 2 - b, chans, 8), :])
                winb[b * chans:(b + 1) * chans, a * hidden:(a + 1) * hidden] = high
                winb[taps + b * chans:taps + (b + 1) * chans, a * hidden:(a + 1) * hidden] = low
        for a in range(3):
            put_wide(woutb, a, jnp.concatenate(
                [w_out_ref[:, tap_block(2 - a, 2 - b, hidden, 128)] for b in range(3)], axis=0))

    def put_line(t, line):
        for b in range(3):
            high, low = split(shifted(line, b))
            at = t * depth + b * chans
            s_high[at:at + chans, :] = high
            s_low[at:at + chans, :] = low

    def joined(ref, size, lines):
        return jnp.concatenate([ref[t * size:(t + 1) * size, :] for t in lines], axis=1)

    def widen(weights, parts):
        sums = {}
        for a, lines in parts:
            high = joined(s_high, depth, lines)
            low = joined(s_low, depth, lines)
            both = dot(weights[a], high)
            total = both[0:hidden] + both[hidden:2 * hidden] + dot(weights[a, 0:hidden, :], low)
            for n, t in enumerate(lines):
                line = total[:, n * cols:(n + 1) * cols]
                sums[t - a] = line if t - a not in sums else sums[t - a] + line
        return sums

    def narrow(weights, parts):
        sums = {}
        for a, outs in parts:
            lines = [i + a for i in outs]
            at = a * hidden
            both = dot(weights[:, at:at + hidden], joined(h_high, hidden, lines))
            total = both[0:taps] + both[taps:2 * taps] + dot(
                weights[0:taps, at:at + hidden], joined(h_low, hidden, lines))
            for n, i in enumerate(outs):
                line = total[:, n * cols:(n + 1) * cols]
                sums[i] = line if i not in sums else sums[i] + line
        return sums

    def put_hidden(j, value):
        if j == 0:
            value = jnp.where(has_slow, value, 0.0)
        high, low = split(value)
        h_high[j * hidden:(j + 1) * hidden, :] = high
        h_low[j * hidden:(j + 1) * hidden, :] = low

    def bend(step, j, value):
        value = value + bias[...]
        inner = jnp.tanh(gelu_scale * (value + gelu_cubic * value * value * value))
        put_hidden(j, 0.5 * value * (1.0 + inner))
        slope[step, j] = 0.5 * (1.0 + inner) + 0.5 * value * (1.0 - inner * inner) * (
            gelu_scale * (1.0 + 3.0 * gelu_cubic * value * value))

    def unbend(step, j, value):
        put_hidden(j, value * slope[step, j])

    def own_part(weights, own):
        for i in range(rows):
            put_line(i + 2, own[i])
        for j, line in widen(weights, [(a, range(2, rows + 2)) for a in range(3)]).items():
            before[j] = line

    def convolve(wide, slim, n, own, act):
        pltpu.make_async_copy(halo.at[n, 1], halo.at[n, 1], fast_recv.at[n]).wait()
        for far in range(2):
            put_line(rows + 2 + far, halo[n, 1, far])
        sums = widen(wide, [(2, (rows + 2, rows + 3)), (1, (rows + 2,))])
        for j in range(2, rows + 2):
            act(j, before[j] + sums[j] if j in sums else before[j])
        early = [(a, [i for i in range(rows) if i + a >= 2]) for a in (2, 1, 0)]
        for i, line in narrow(slim, [part for part in early if part[1]]).items():
            narrowed[i] = line
        slow_wait(n, own, 0)
        put_line(1, halo[n, 0, 0])
        sums = widen(wide, [(0, (1,)), (1, (1,))])
        before[0] += sums[0]
        act(1, before[1] + sums[1])
        slow_wait(n, own, 1)
        put_line(0, halo[n, 0, 1])
        act(0, before[0] + widen(wide, [(0, (0,))])[0])
        sums = narrow(slim, [(1, (0,)), (0, (0, 1))])
        result = []
        for i in range(rows):
            line = narrowed[i] + sums[i] if i in sums else narrowed[i]
            result.append(sum(shifted(line[b * chans:(b + 1) * chans], b) for b in range(3)))
        return result

    def fold(value):
        return sum(value[8 * i:8 * i + 8] for i in range(chans // 8))

    def loss_terms(step, i):
        weight = jnp.where(odd == 1, lat_ref[0:1, rows - 1 - i:rows - i], lat_ref[0:1, i:i + 1])
        mine = fields[step, i]
        error = mine - target_ref[step, i]
        square = error * error + smooth_width * smooth_width
        inverse = lax.rsqrt(square)
        direct = square * inverse
        gradient = error * inverse
        summed = jnp.full(mine.shape, smooth_width, F32)
        slopes = jnp.zeros_like(mine)
        for k in range(1, members):
            spread = mine - others[step, k - 1, i]
            square = spread * spread + smooth_width * smooth_width
            inverse = lax.rsqrt(square)
            summed = summed + square * inverse
            slopes = slopes + spread * inverse
        loss_grad[step, i] = weight * (gradient - slopes / (members - 1))
        return weight * fold(direct - summed / (2.0 * (members - 1)))

    for step in range(steps):
        own = x_ref if step == 0 else fields.at[step - 1]
        if step == 0:
            front_weights()
        own_part(win, own)
        if step == 0:
            narrow_weights()
        else:
            back_weights()
        if step < len(rounds):
            reached(step)
            if step + 1 < len(rounds):
                reach_out(step + 1)
        change = convolve(win, wout, step, own, functools.partial(bend, step))
        for i in range(rows):
            fields[step, i] = own[i] + change[i]
        if step < steps - 1:
            halo_start(step + 1, fields.at[step])
        if step == steps - 1:
            for r in range(steps, len(rounds)):
                reached(r)
                if r + 1 < len(rounds):
                    reach_out(r + 1)
        for i in range(rows):
            for k in peers:
                to_member(step, k, i).start()

    arrive(4)
    arrive(5)
    partial = jnp.zeros((8, cols), F32)
    for step in range(steps):
        for i in range(rows):
            landed = others.at[step, :, i]
            pltpu.make_async_copy(landed, landed, other_recv.at[step, i]).wait()
            partial = partial + loss_terms(step, i)
            if step == steps - 1:
                grads[step, i] = loss_grad[step, i]
                if i < 2:
                    slow_start(steps, grads.at[step], (i,))
                if rows - 1 - i < 2:
                    to_fast(steps, grads.at[step], rows - 1 - i).start()

    me = me_m * bands + me_l
    parts[me] = jnp.sum(partial, axis=0, keepdims=True)
    for n in range(1, members * bands):
        pltpu.make_async_remote_copy(
            src_ref=parts.at[me], dst_ref=parts.at[me], send_sem=part_send.at[0], recv_sem=part_recv.at[0],
            device_id={"member": lax.rem(me_m + n // bands, members), "lat": lax.rem(me_l + n % bands, bands)},
            device_id_type=MESH).start()

    for step in range(steps - 1, -1, -1):
        n = 2 * steps - 1 - step
        own = grads.at[step]
        if step < steps - 1:
            for i in range(rows):
                grads[step, i] = grads[step + 1, i] + change[i] + loss_grad[step, i]
            halo_start(n, own)
        own_part(woutb, own)
        change = convolve(woutb, winb, n, own, functools.partial(unbend, step))

    for i in range(rows):
        grad_ref[mirrored(i, rows - 1)] = grads[0, i] + change[i]
    sent = parts.at[0:members * bands - 1]
    pltpu.make_async_copy(sent, sent, part_recv.at[0]).wait()
    total = jnp.sum(parts[...], axis=0)
    count = members * steps * rows * bands * chans * cols
    loss_ref[...] = jnp.full(loss_ref.shape, jnp.sum(total) / count, F32)
    pltpu.make_async_copy(sent, sent, part_send.at[0]).wait()
    pltpu.make_async_copy(others, others, other_send.at[0]).wait()
    pltpu.make_async_copy(halo.at[:, 1], halo.at[:, 1], halo_send.at[1]).wait()

    @pl.when(has_slow)
    def _():
        pltpu.make_async_copy(halo.at[:, 0], halo.at[:, 0], halo_send.at[0]).wait()


def deliver(grad_vmem, loss_vmem, grad_hbm, loss_hbm, loss_smem, sem):
    gradient = pltpu.make_async_copy(grad_vmem, grad_hbm, sem.at[0])
    loss = pltpu.make_async_copy(loss_smem, loss_hbm, sem.at[1])
    gradient.start()
    loss_smem[0, 0] = loss_vmem[0, 0]
    loss.start()
    loss.wait()
    gradient.wait()


def on_device(members, bands, initial_states, targets, lat_weight, weight_in, weight_out, hidden_bias):
    steps, rows, chans, cols = targets.shape
    hidden = weight_in.shape[0]
    taps = 3 * chans
    depth = -(-taps // 256) * 256
    deep = 3 * hidden
    vmem = pl.BlockSpec(memory_space=pltpu.VMEM)
    dma = pltpu.SemaphoreType.DMA
    gradient, loss = pl.pallas_call(
        functools.partial(kernel, members, bands),
        out_shape=(pltpu.VMEM((rows, chans, cols), F32), pltpu.VMEM((8, cols), F32)),
        in_specs=[pl.BlockSpec(memory_space=pltpu.HBM)] * 6,
        out_specs=(vmem, vmem),
        scratch_shapes=[
            pltpu.VMEM((rows, chans, cols), F32),
            pltpu.VMEM(targets.shape, F32),
            pltpu.VMEM((1, rows), F32),
            pltpu.VMEM((3 * taps, hidden), F32),
            pltpu.VMEM((chans, 3 * deep), F32),
            pltpu.VMEM((1, hidden), F32),
            dma((6,)),
            pltpu.VMEM((2 * steps, 2, 2, chans, cols), F32),
            pltpu.VMEM((steps, members - 1, rows, chans, cols), F32),
            pltpu.VMEM((members * bands, 1, cols), F32),
            pltpu.VMEM((steps, rows, chans, cols), F32),
            pltpu.VMEM((steps, rows, chans, cols), F32),
            pltpu.VMEM((3, 2 * hidden, depth), BF16),
            pltpu.VMEM((2 * taps, deep), BF16),
            pltpu.VMEM((2 * taps, deep), BF16),
            pltpu.VMEM((3, 2 * hidden, depth), BF16),
            pltpu.VMEM((depth, hidden), F32),
            pltpu.VMEM(((rows + 4) * depth, cols), BF16),
            pltpu.VMEM(((rows + 4) * depth, cols), BF16),
            pltpu.VMEM(((rows + 2) * hidden, cols), BF16),
            pltpu.VMEM(((rows + 2) * hidden, cols), BF16),
            pltpu.VMEM((rows + 2, hidden, cols), F32),
            pltpu.VMEM((steps, rows + 2, hidden, cols), F32),
            pltpu.VMEM((rows, taps, cols), F32),
            pltpu.VMEM((steps, rows, chans, cols), F32),
            pltpu.VMEM((hidden, cols), F32),
            dma((2,)), dma((2 * steps, 2)), dma((2 * steps,)),
            dma((1,)), dma((steps, rows)),
            dma((1,)), dma((1,)),
            pltpu.SemaphoreType.REGULAR((max(1, (bands - 2).bit_length()),)),
        ],
        compiler_params=pltpu.CompilerParams(collective_id=0, has_side_effects=True, vmem_limit_bytes=24 * 2**20),
    )(
        *(pltpu.with_memory_space_constraint(value, pltpu.HBM) for value in (
            initial_states.reshape(rows, chans, cols), targets, lat_weight.reshape(1, rows),
            weight_in.T, weight_out, hidden_bias.reshape(1, hidden)))
    )
    anywhere = pl.BlockSpec(memory_space=pl.ANY)
    gradient, loss = pl.pallas_call(
        deliver,
        out_shape=(jax.ShapeDtypeStruct((rows, chans, cols), F32), jax.ShapeDtypeStruct((1, 1), F32)),
        in_specs=[vmem, vmem],
        out_specs=(anywhere, anywhere),
        scratch_shapes=[pltpu.SMEM((1, 1), F32), dma((2,))],
    )(*(pltpu.with_memory_space_constraint(value, pltpu.VMEM) for value in (gradient, loss)))
    return gradient.reshape(initial_states.shape), loss.reshape(())


def solution(mesh):
    placed = (P("member", "lat", None, None), P(None, "lat", None, None), P("lat"), P(), P(), P())
    return jax.shard_map(
        functools.partial(on_device, mesh.shape["member"], mesh.shape["lat"]),
        mesh=mesh,
        in_specs=placed,
        out_specs=(P("member", "lat", None, None), P()),
        check_vma=False,
    )
```

```python
import functools

import jax
import jax.numpy as jnp
from jax import lax
from jax.experimental import pallas as pl
from jax.experimental.pallas import tpu as pltpu
from jax.sharding import PartitionSpec as P

smooth_width = 0.1
gelu_scale = 0.7978845608028654
gelu_cubic = 0.044715
MESH = pl.DeviceIdType.MESH
F32 = jnp.float32
BF16 = jnp.bfloat16


def split(value):
    high = value.astype(BF16)
    low = (value - high.astype(F32)).astype(BF16)
    return high, low


def shifted(value, tap):
    if tap == 1:
        return value
    columns = value.shape[-1]
    lane = lax.broadcasted_iota(jnp.int32, value.shape, 1)
    if tap == 0:
        return jnp.where(lane == 0, 0.0, pltpu.roll(value, 1, 1))
    return jnp.where(lane == columns - 1, 0.0, pltpu.roll(value, columns - 1, 1))


def dot(left, right):
    return jnp.dot(left, right, preferred_element_type=F32)


def kernel(
    members, bands,
    x_hbm, target_hbm, lat_hbm, w_in_hbm, w_out_hbm, bias_hbm,
    grad_ref, loss_ref,
    x_ref, target_ref, lat_ref, w_in_ref, w_out_ref, bias_ref, fetch_sem,
    halo, others, parts, fields, grads,
    win, winb, wout, woutb, tall, s_high, s_low, h_high, h_low, before, slope, bent, narrowed, edge, loss_grad, bias,
    halo_send, slow_recv, fast_recv, other_send, other_recv, part_send, part_recv, reach,
):
    steps, rows, chans, cols = target_ref.shape
    hidden = w_in_ref.shape[1]
    taps = 3 * chans
    depth = win.shape[2]
    me_m = lax.axis_index("member")
    me_l = lax.axis_index("lat")
    odd = lax.rem(me_l, 2)
    slow = me_l - 1 + 2 * odd
    fast = me_l + 1 - 2 * odd
    has_slow = jnp.logical_and(slow >= 0, slow < bands)
    slow = jnp.clip(slow, 0, bands - 1)

    def mirrored(n, last):
        return n + odd * (last - 2 * n)

    def fetch(n, copies):
        return [pltpu.make_async_copy(source, target, fetch_sem.at[n]) for source, target in copies]

    mirror = [mirrored(i, rows - 1) for i in range(rows)]
    fetches = [
        fetch(0, [(x_hbm.at[mirror[i]], x_ref.at[i]) for i in range(rows)]),
        fetch(1, [(w_in_hbm, w_in_ref)]),
        fetch(2, [(bias_hbm, bias_ref)]),
        fetch(3, [(w_out_hbm, w_out_ref)]),
        fetch(4, [(target_hbm.at[:, mirror[i]], target_ref.at[:, i]) for i in range(rows)]),
        fetch(5, [(lat_hbm, lat_ref)]),
    ]
    arrivals = [x_ref, w_in_ref, bias_ref, w_out_ref, target_ref, lat_ref]

    def arrive(n):
        pltpu.make_async_copy(arrivals[n], arrivals[n], fetch_sem.at[n]).wait()

    for copy in fetches[0]:
        copy.start()
    barrier = pltpu.get_barrier_semaphore()
    for k in range(1, members):
        pl.semaphore_signal(barrier, inc=1, device_id={"member": lax.rem(me_m + k, members)}, device_id_type=MESH)
    pl.semaphore_signal(barrier, inc=1, device_id={"lat": fast}, device_id_type=MESH)

    @pl.when(has_slow)
    def _():
        pl.semaphore_signal(barrier, inc=1, device_id={"lat": slow}, device_id_type=MESH)

    for copies in fetches[1:]:
        for copy in copies:
            copy.start()

    def to_slow(n, source, far):
        return pltpu.make_async_remote_copy(
            src_ref=source.at[far], dst_ref=halo.at[n, 0, far],
            send_sem=halo_send.at[0], recv_sem=slow_recv.at[n, far],
            device_id={"lat": slow}, device_id_type=MESH)

    def to_fast(n, source, far):
        return pltpu.make_async_remote_copy(
            src_ref=source.at[rows - 1 - far], dst_ref=halo.at[n, 1, far],
            send_sem=halo_send.at[1], recv_sem=fast_recv.at[n],
            device_id={"lat": fast}, device_id_type=MESH)

    def send_row(n, source, i):
        if i < 2:
            @pl.when(has_slow)
            def _():
                to_slow(n, source, i).start()

        if rows - 1 - i < 2:
            to_fast(n, source, rows - 1 - i).start()

    def peer(k):
        if members & (members - 1):
            return lax.rem(me_m + k, members)
        result, bit = 0, 1
        while bit < members:
            mine = lax.rem(me_m // bit, 2)
            result = result + bit * (1 - mine if k & bit else mine)
            bit *= 2
        return result

    peers = sorted(range(1, members), key=lambda k: -bin(k).count("1"))

    def to_member(step, k, i):
        return pltpu.make_async_remote_copy(
            src_ref=fields.at[step, i], dst_ref=others.at[step, k - 1, i],
            send_sem=other_send.at[0], recv_sem=other_recv.at[step, i],
            device_id={"member": peer(k)}, device_id_type=MESH)

    rounds = [1]
    while 2 * rounds[-1] < bands - 1:
        rounds.append(2 * rounds[-1])

    def reach_out(r):
        for far in (me_l - rounds[r], me_l + rounds[r]):
            @pl.when(jnp.logical_and(far >= 0, far < bands))
            def _():
                pl.semaphore_signal(
                    reach.at[r], inc=1, device_id={"lat": jnp.clip(far, 0, bands - 1)}, device_id_type=MESH)

    def reached(r):
        below = (me_l >= rounds[r]).astype(jnp.int32)
        above = (me_l + rounds[r] < bands).astype(jnp.int32)
        pl.semaphore_wait(reach.at[r], below + above)

    arrive(0)
    pl.semaphore_wait(barrier, members + has_slow.astype(jnp.int32))
    for i in range(rows):
        send_row(0, x_ref, i)
    reach_out(0)

    def put_wide(target, a, block):
        tall[0:taps, :] = block
        high, low = split(tall[...].T)
        target[a, 0:hidden] = high
        target[a, hidden:2 * hidden] = low

    def tap_rows(a):
        return pl.ds(pl.multiple_of(mirrored(a, 2) * taps, 8), taps)

    def tap_block(a, b, size, unit):
        return pl.ds(pl.multiple_of((3 * mirrored(a, 2) + b) * size, unit), size)

    def front_weights():
        arrive(1)
        arrive(2)
        tall[taps:, :] = jnp.zeros((depth - taps, hidden), F32)
        for a in range(3):
            put_wide(win, a, w_in_ref[tap_rows(a), :])
        bias[...] = jnp.broadcast_to(bias_ref[...], (cols, hidden)).T
        for t in range(rows + 4):
            s_high[t * depth + taps:(t + 1) * depth, :] = jnp.zeros((depth - taps, cols), BF16)
            s_low[t * depth + taps:(t + 1) * depth, :] = jnp.zeros((depth - taps, cols), BF16)

    def narrow_weights():
        arrive(3)
        for a in range(3):
            for b in range(3):
                high, low = split(w_out_ref[:, tap_block(a, b, hidden, 128)])
                wout[a, b * chans:(b + 1) * chans, :] = high
                wout[a, taps + b * chans:taps + (b + 1) * chans, :] = low

    def back_weights():
        for a in range(3):
            for b in range(3):
                high, low = split(w_in_ref[tap_block(2 - a, 2 - b, chans, 8), :])
                winb[a, b * chans:(b + 1) * chans, :] = high
                winb[a, taps + b * chans:taps + (b + 1) * chans, :] = low
        for a in range(3):
            put_wide(woutb, a, jnp.concatenate(
                [w_out_ref[:, tap_block(2 - a, 2 - b, hidden, 128)] for b in range(3)], axis=0))

    def put_line(t, line):
        for b in range(3):
            high, low = split(shifted(line, b))
            at = t * depth + b * chans
            s_high[at:at + chans, :] = high
            s_low[at:at + chans, :] = low

    def joined(ref, size, lines):
        return jnp.concatenate([ref[t * size:(t + 1) * size, :] for t in lines], axis=1)

    def widen(weights, parts):
        sums = {}
        for a, lines in parts:
            high = joined(s_high, depth, lines)
            low = joined(s_low, depth, lines)
            both = dot(weights[a], high)
            total = both[0:hidden] + both[hidden:2 * hidden] + dot(weights[a, 0:hidden, :], low)
            for n, t in enumerate(lines):
                line = total[:, n * cols:(n + 1) * cols]
                sums[t - a] = line if t - a not in sums else sums[t - a] + line
        return sums

    def half(weights, a, high, low):
        both = jnp.concatenate([high, low], axis=1)
        size = weights.shape[1] // 2
        middle = -(-size // 32) * 16
        lines = []
        for first, last in ((0, middle), (middle, size)):
            line = dot(weights[a, first:last, :], both) + dot(weights[a, size + first:size + last, :], both)
            lines.append(line[:, 0:cols] + line[:, cols:2 * cols])
        return jnp.concatenate(lines, axis=0)

    def widen_line(weights, a, t):
        at = t * depth
        return half(weights, a, s_high[at:at + depth, :], s_low[at:at + depth, :])

    def narrow_line(weights, a, j):
        at = j * hidden
        return half(weights, a, h_high[at:at + hidden, :], h_low[at:at + hidden, :])

    def collect(total):
        return sum(shifted(total[b * chans:(b + 1) * chans], b) for b in range(3))

    def narrow(weights, parts):
        sums = {}
        for a, outs in parts:
            lines = [i + a for i in outs]
            both = dot(weights[a], joined(h_high, hidden, lines))
            total = both[0:taps] + both[taps:2 * taps] + dot(weights[a, 0:taps, :], joined(h_low, hidden, lines))
            for n, i in enumerate(outs):
                line = total[:, n * cols:(n + 1) * cols]
                sums[i] = line if i not in sums else sums[i] + line
        return sums

    def put_hidden(j, value):
        high, low = split(value)
        h_high[j * hidden:(j + 1) * hidden, :] = high
        h_low[j * hidden:(j + 1) * hidden, :] = low

    def bend(step, j, value):
        value = value + bias[...]
        inner = jnp.tanh(gelu_scale * (value + gelu_cubic * value * value * value))
        put_hidden(j, 0.5 * value * (1.0 + inner))
        slope[step, j] = value
        bent[step, j] = inner

    def slopes_of(step):
        for j in range(rows + 2):
            value, inner = slope[step, j], bent[step, j]
            slope[step, j] = 0.5 * (1.0 + inner) + 0.5 * value * (1.0 - inner * inner) * (
                gelu_scale * (1.0 + 3.0 * gelu_cubic * value * value))

    def unbend(step, j, value):
        put_hidden(j, value * slope[step, j])

    def own_part(wide, slim, own, act):
        for i in range(rows):
            put_line(i + 2, own[i])
        for j, line in widen(wide, [(a, range(2, rows + 2)) for a in range(3)]).items():
            before[j] = line

        @pl.when(jnp.logical_not(has_slow))
        def _():
            act(1, before[1])
            for i in range(2):
                edge[i] = narrow_line(slim, 1 - i, 1)

    def convolve(wide, slim, n, own, act, finish, pause=lambda: None):
        pltpu.make_async_copy(halo.at[n, 1], halo.at[n, 1], fast_recv.at[n]).wait()
        for far in range(2):
            put_line(rows + 2 + far, halo[n, 1, far])
        sums = widen(wide, [(2, (rows + 2, rows + 3)), (1, (rows + 2,))])
        for j in range(2, rows + 2):
            act(j, before[j] + sums[j] if j in sums else before[j])
        ready = [(a, [i for i in range(rows) if i + a >= 2]) for a in (2, 1, 0)]
        for i, line in narrow(slim, [part for part in ready if part[1]]).items():
            if i < 2:
                narrowed[i] = line
            else:
                finish(i, collect(line))
        pause()

        @pl.when(jnp.logical_not(has_slow))
        def _():
            for i in (1, 0):
                finish(i, collect(narrowed[i] + edge[i]))

        @pl.when(has_slow)
        def _():
            to_slow(n, own, 1).wait_recv()
            put_line(0, halo[n, 0, 1])
            before[0] += widen_line(wide, 0, 0)
            to_slow(n, own, 0).wait_recv()
            put_line(1, halo[n, 0, 0])
            act(1, before[1] + widen_line(wide, 0, 1))
            act(0, before[0] + widen_line(wide, 1, 1))
            finish(1, collect(narrowed[1] + narrow_line(slim, 0, 1)))
            finish(0, collect(narrowed[0] + narrow_line(slim, 1, 1) + narrow_line(slim, 0, 0)))

    def fold(value):
        return sum(value[8 * i:8 * i + 8] for i in range(chans // 8))

    def loss_terms(step, i):
        weight = jnp.where(odd == 1, lat_ref[0:1, rows - 1 - i:rows - i], lat_ref[0:1, i:i + 1])
        mine = fields[step, i]
        error = mine - target_ref[step, i]
        square = error * error + smooth_width * smooth_width
        inverse = lax.rsqrt(square)
        direct = square * inverse
        gradient = error * inverse
        summed = jnp.full(mine.shape, smooth_width, F32)
        slopes = jnp.zeros_like(mine)
        for k in range(1, members):
            spread = mine - others[step, k - 1, i]
            square = spread * spread + smooth_width * smooth_width
            inverse = lax.rsqrt(square)
            summed = summed + square * inverse
            slopes = slopes + spread * inverse
        loss_grad[step, i] = weight * (gradient - slopes / (members - 1))
        return weight * fold(direct - summed / (2.0 * (members - 1)))

    for step in range(steps):
        own = x_ref if step == 0 else fields.at[step - 1]
        if step == 0:
            front_weights()
            narrow_weights()
        act = functools.partial(bend, step)
        own_part(win, wout, own, act)
        if step > 0:
            back_weights()
        if step < len(rounds):
            reached(step)
            if step + 1 < len(rounds):
                reach_out(step + 1)

        def advance(i, change):
            fields[step, i] = own[i] + change
            if step < steps - 1:
                send_row(step + 1, fields.at[step], i)
            else:
                for k in peers:
                    to_member(step, k, i).start()

        def pause():
            if step == steps - 1:
                for r in range(steps, len(rounds)):
                    reached(r)
                    if r + 1 < len(rounds):
                        reach_out(r + 1)

        convolve(win, wout, step, own, act, advance, pause)
        if step < steps - 1:
            for i in range(rows):
                for k in peers:
                    to_member(step, k, i).start()

    for step in range(steps):
        slopes_of(step)
    arrive(4)
    arrive(5)
    partial = jnp.zeros((8, cols), F32)
    for step in range(steps):
        for i in reversed(range(rows)):
            landed = others.at[step, :, i]
            pltpu.make_async_copy(landed, landed, other_recv.at[step, i]).wait()
            partial = partial + loss_terms(step, i)
            if step == steps - 1:
                grads[step, i] = loss_grad[step, i]
                send_row(steps, grads.at[step], i)

    me = me_m * bands + me_l
    parts[me] = jnp.sum(partial, axis=0, keepdims=True)

    for step in range(steps - 1, -1, -1):
        n = 2 * steps - 1 - step
        own = grads.at[step]

        def retreat(i, change):
            if step > 0:
                grads[step - 1, i] = grads[step, i] + change + loss_grad[step - 1, i]
                send_row(n + 1, grads.at[step - 1], i)
            else:
                grad_ref[mirror[i]] = grads[0, i] + change

        act = functools.partial(unbend, step)
        own_part(woutb, winb, own, act)
        if step == steps - 1:
            for k in range(1, members * bands):
                pltpu.make_async_remote_copy(
                    src_ref=parts.at[me], dst_ref=parts.at[me], send_sem=part_send.at[0], recv_sem=part_recv.at[0],
                    device_id={"member": lax.rem(me_m + k // bands, members), "lat": lax.rem(me_l + k % bands, bands)},
                    device_id_type=MESH).start()
        convolve(woutb, winb, n, own, act, retreat)

    sent = parts.at[0:members * bands - 1]
    pltpu.make_async_copy(sent, sent, part_recv.at[0]).wait()
    total = jnp.sum(parts[...], axis=0)
    count = members * steps * rows * bands * chans * cols
    loss_ref[...] = jnp.full(loss_ref.shape, jnp.sum(total) / count, F32)
    pltpu.make_async_copy(sent, sent, part_send.at[0]).wait()
    pltpu.make_async_copy(others, others, other_send.at[0]).wait()
    pltpu.make_async_copy(halo.at[:, 1], halo.at[:, 1], halo_send.at[1]).wait()

    @pl.when(has_slow)
    def _():
        pltpu.make_async_copy(halo.at[:, 0], halo.at[:, 0], halo_send.at[0]).wait()


def deliver(grad_vmem, loss_vmem, grad_hbm, loss_hbm, loss_smem, sem):
    gradient = pltpu.make_async_copy(grad_vmem, grad_hbm, sem.at[0])
    loss = pltpu.make_async_copy(loss_smem, loss_hbm, sem.at[1])
    gradient.start()
    loss_smem[0, 0] = loss_vmem[0, 0]
    loss.start()
    loss.wait()
    gradient.wait()


def on_device(members, bands, initial_states, targets, lat_weight, weight_in, weight_out, hidden_bias):
    steps, rows, chans, cols = targets.shape
    hidden = weight_in.shape[0]
    taps = 3 * chans
    depth = -(-taps // 256) * 256
    deep = 3 * hidden
    vmem = pl.BlockSpec(memory_space=pltpu.VMEM)
    dma = pltpu.SemaphoreType.DMA
    gradient, loss = pl.pallas_call(
        functools.partial(kernel, members, bands),
        out_shape=(pltpu.VMEM((rows, chans, cols), F32), pltpu.VMEM((8, cols), F32)),
        in_specs=[pl.BlockSpec(memory_space=pltpu.HBM)] * 6,
        out_specs=(vmem, vmem),
        scratch_shapes=[
            pltpu.VMEM((rows, chans, cols), F32),
            pltpu.VMEM(targets.shape, F32),
            pltpu.VMEM((1, rows), F32),
            pltpu.VMEM((3 * taps, hidden), F32),
            pltpu.VMEM((chans, 3 * deep), F32),
            pltpu.VMEM((1, hidden), F32),
            dma((6,)),
            pltpu.VMEM((2 * steps, 2, 2, chans, cols), F32),
            pltpu.VMEM((steps, members - 1, rows, chans, cols), F32),
            pltpu.VMEM((members * bands, 1, cols), F32),
            pltpu.VMEM((steps, rows, chans, cols), F32),
            pltpu.VMEM((steps, rows, chans, cols), F32),
            pltpu.VMEM((3, 2 * hidden, depth), BF16),
            pltpu.VMEM((3, 2 * taps, hidden), BF16),
            pltpu.VMEM((3, 2 * taps, hidden), BF16),
            pltpu.VMEM((3, 2 * hidden, depth), BF16),
            pltpu.VMEM((depth, hidden), F32),
            pltpu.VMEM(((rows + 4) * depth, cols), BF16),
            pltpu.VMEM(((rows + 4) * depth, cols), BF16),
            pltpu.VMEM(((rows + 2) * hidden, cols), BF16),
            pltpu.VMEM(((rows + 2) * hidden, cols), BF16),
            pltpu.VMEM((rows + 2, hidden, cols), F32),
            pltpu.VMEM((steps, rows + 2, hidden, cols), F32),
            pltpu.VMEM((steps, rows + 2, hidden, cols), F32),
            pltpu.VMEM((2, taps, cols), F32),
            pltpu.VMEM((2, taps, cols), F32),
            pltpu.VMEM((steps, rows, chans, cols), F32),
            pltpu.VMEM((hidden, cols), F32),
            dma((2,)), dma((2 * steps, 2)), dma((2 * steps,)),
            dma((1,)), dma((steps, rows)),
            dma((1,)), dma((1,)),
            pltpu.SemaphoreType.REGULAR((max(1, (bands - 2).bit_length()),)),
        ],
        compiler_params=pltpu.CompilerParams(collective_id=0, has_side_effects=True, vmem_limit_bytes=24 * 2**20),
    )(
        *(pltpu.with_memory_space_constraint(value, pltpu.HBM) for value in (
            initial_states.reshape(rows, chans, cols), targets, lat_weight.reshape(1, rows),
            weight_in.T, weight_out, hidden_bias.reshape(1, hidden)))
    )
    anywhere = pl.BlockSpec(memory_space=pl.ANY)
    gradient, loss = pl.pallas_call(
        deliver,
        out_shape=(jax.ShapeDtypeStruct((rows, chans, cols), F32), jax.ShapeDtypeStruct((1, 1), F32)),
        in_specs=[vmem, vmem],
        out_specs=(anywhere, anywhere),
        scratch_shapes=[pltpu.SMEM((1, 1), F32), dma((2,))],
    )(*(pltpu.with_memory_space_constraint(value, pltpu.VMEM) for value in (gradient, loss)))
    return gradient.reshape(initial_states.shape), loss.reshape(())


def solution(mesh):
    placed = (P("member", "lat", None, None), P(None, "lat", None, None), P("lat"), P(), P(), P())
    return jax.shard_map(
        functools.partial(on_device, mesh.shape["member"], mesh.shape["lat"]),
        mesh=mesh,
        in_specs=placed,
        out_specs=(P("member", "lat", None, None), P()),
        check_vma=False,
    )
```

```python
import functools

import jax
import jax.numpy as jnp
from jax import lax
from jax.experimental import pallas as pl
from jax.experimental.pallas import tpu as pltpu
from jax.sharding import PartitionSpec as P

smooth_width = 0.1
gelu_scale = 0.7978845608028654
gelu_cubic = 0.044715
MESH = pl.DeviceIdType.MESH
F32 = jnp.float32
BF16 = jnp.bfloat16


def split(value):
    high = value.astype(BF16)
    low = (value - high.astype(F32)).astype(BF16)
    return high, low


def shifted(value, tap):
    if tap == 1:
        return value
    columns = value.shape[-1]
    lane = lax.broadcasted_iota(jnp.int32, value.shape, 1)
    if tap == 0:
        return jnp.where(lane == 0, 0.0, pltpu.roll(value, 1, 1))
    return jnp.where(lane == columns - 1, 0.0, pltpu.roll(value, columns - 1, 1))


def dot(left, right):
    return jnp.dot(left, right, preferred_element_type=F32)


def kernel(
    members, bands,
    x_hbm, target_hbm, lat_hbm, w_in_hbm, w_out_hbm, bias_hbm,
    grad_ref, loss_ref,
    x_ref, target_ref, lat_ref, w_in_ref, w_out_ref, bias_ref, fetch_sem,
    halo, everyone, parts, fields, grads,
    win, winb, wout, woutb, tall, s_high, s_low, h_high, h_low, before, slope, bent, narrowed, edge, loss_grad, bias,
    halo_send, slow_recv, fast_recv, other_send, other_recv, part_send, part_recv, reach,
):
    steps, rows, chans, cols = target_ref.shape
    hidden = w_in_ref.shape[1]
    taps = 3 * chans
    depth = win.shape[2]
    me_m = lax.axis_index("member")
    me_l = lax.axis_index("lat")
    odd = lax.rem(me_l, 2)
    slow = me_l - 1 + 2 * odd
    fast = me_l + 1 - 2 * odd
    has_slow = jnp.logical_and(slow >= 0, slow < bands)
    slow = jnp.clip(slow, 0, bands - 1)

    def mirrored(n, last):
        return n + odd * (last - 2 * n)

    def fetch(n, copies):
        return [pltpu.make_async_copy(source, target, fetch_sem.at[n]) for source, target in copies]

    mirror = [mirrored(i, rows - 1) for i in range(rows)]
    fetches = [
        fetch(0, [(x_hbm.at[mirror[i]], x_ref.at[i]) for i in range(rows)]),
        fetch(1, [(w_in_hbm, w_in_ref)]),
        fetch(2, [(bias_hbm, bias_ref)]),
        fetch(3, [(w_out_hbm, w_out_ref)]),
        fetch(4, [(target_hbm.at[:, mirror[i]], target_ref.at[:, i]) for i in range(rows)]),
        fetch(5, [(lat_hbm, lat_ref)]),
    ]
    arrivals = [x_ref, w_in_ref, bias_ref, w_out_ref, target_ref, lat_ref]

    def arrive(n):
        pltpu.make_async_copy(arrivals[n], arrivals[n], fetch_sem.at[n]).wait()

    for copy in fetches[0]:
        copy.start()
    barrier = pltpu.get_barrier_semaphore()
    for k in range(1, members):
        pl.semaphore_signal(barrier, inc=1, device_id={"member": lax.rem(me_m + k, members)}, device_id_type=MESH)
    pl.semaphore_signal(barrier, inc=1, device_id={"lat": fast}, device_id_type=MESH)

    @pl.when(has_slow)
    def _():
        pl.semaphore_signal(barrier, inc=1, device_id={"lat": slow}, device_id_type=MESH)

    for copies in fetches[1:]:
        for copy in copies:
            copy.start()

    def to_slow(n, source, far):
        return pltpu.make_async_remote_copy(
            src_ref=source.at[far], dst_ref=halo.at[n, 0, far],
            send_sem=halo_send.at[0], recv_sem=slow_recv.at[n, far],
            device_id={"lat": slow}, device_id_type=MESH)

    def to_fast(n, source, far):
        return pltpu.make_async_remote_copy(
            src_ref=source.at[rows - 1 - far], dst_ref=halo.at[n, 1, far],
            send_sem=halo_send.at[1], recv_sem=fast_recv.at[n],
            device_id={"lat": fast}, device_id_type=MESH)

    def send_row(n, source, i):
        if i < 2:
            @pl.when(has_slow)
            def _():
                to_slow(n, source, i).start()

        if rows - 1 - i < 2:
            to_fast(n, source, rows - 1 - i).start()

    def peer(k):
        if members & (members - 1):
            return lax.rem(me_m + k, members)
        result, bit = 0, 1
        while bit < members:
            mine = lax.rem(me_m // bit, 2)
            result = result + bit * (1 - mine if k & bit else mine)
            bit *= 2
        return result

    peers = sorted(range(1, members), key=lambda k: -bin(k).count("1"))

    def to_member(step, k, i):
        return pltpu.make_async_remote_copy(
            src_ref=everyone.at[step, me_m, i], dst_ref=everyone.at[step, me_m, i],
            send_sem=other_send.at[0], recv_sem=other_recv.at[step, i],
            device_id={"member": peer(k)}, device_id_type=MESH)

    rounds = [1]
    while 2 * rounds[-1] < bands - 1:
        rounds.append(2 * rounds[-1])

    def reach_out(r):
        for far in (me_l - rounds[r], me_l + rounds[r]):
            @pl.when(jnp.logical_and(far >= 0, far < bands))
            def _():
                pl.semaphore_signal(
                    reach.at[r], inc=1, device_id={"lat": jnp.clip(far, 0, bands - 1)}, device_id_type=MESH)

    def reached(r):
        below = (me_l >= rounds[r]).astype(jnp.int32)
        above = (me_l + rounds[r] < bands).astype(jnp.int32)
        pl.semaphore_wait(reach.at[r], below + above)

    arrive(0)
    pl.semaphore_wait(barrier, members + has_slow.astype(jnp.int32))
    for i in range(rows):
        send_row(0, x_ref, i)
    reach_out(0)

    def put_wide(target, a, block):
        tall[0:taps, :] = block
        high, low = split(tall[...].T)
        target[a, 0:hidden] = high
        target[a, hidden:2 * hidden] = low

    def tap_rows(a):
        return pl.ds(pl.multiple_of(mirrored(a, 2) * taps, 8), taps)

    def tap_block(a, b, size, unit):
        return pl.ds(pl.multiple_of((3 * mirrored(a, 2) + b) * size, unit), size)

    def front_weights():
        arrive(1)
        arrive(2)
        tall[taps:, :] = jnp.zeros((depth - taps, hidden), F32)
        for a in range(3):
            put_wide(win, a, w_in_ref[tap_rows(a), :])
        bias[...] = jnp.broadcast_to(bias_ref[...], (cols, hidden)).T
        for t in range(rows + 4):
            s_high[t * depth + taps:(t + 1) * depth, :] = jnp.zeros((depth - taps, cols), BF16)
            s_low[t * depth + taps:(t + 1) * depth, :] = jnp.zeros((depth - taps, cols), BF16)

    def narrow_weights():
        arrive(3)
        for a in range(3):
            for b in range(3):
                high, low = split(w_out_ref[:, tap_block(a, b, hidden, 128)])
                wout[a, b * chans:(b + 1) * chans, :] = high
                wout[a, taps + b * chans:taps + (b + 1) * chans, :] = low

    def back_weights():
        for a in range(3):
            for b in range(3):
                high, low = split(w_in_ref[tap_block(2 - a, 2 - b, chans, 8), :])
                winb[a, b * chans:(b + 1) * chans, :] = high
                winb[a, taps + b * chans:taps + (b + 1) * chans, :] = low
        for a in range(3):
            put_wide(woutb, a, jnp.concatenate(
                [w_out_ref[:, tap_block(2 - a, 2 - b, hidden, 128)] for b in range(3)], axis=0))

    def put_line(t, line):
        for b in range(3):
            high, low = split(shifted(line, b))
            at = t * depth + b * chans
            s_high[at:at + chans, :] = high
            s_low[at:at + chans, :] = low

    def joined(ref, size, lines):
        return jnp.concatenate([ref[t * size:(t + 1) * size, :] for t in lines], axis=1)

    def widen(weights, parts):
        sums = {}
        for a, lines in parts:
            high = joined(s_high, depth, lines)
            low = joined(s_low, depth, lines)
            both = dot(weights[a], high)
            total = both[0:hidden] + both[hidden:2 * hidden] + dot(weights[a, 0:hidden, :], low)
            for n, t in enumerate(lines):
                line = total[:, n * cols:(n + 1) * cols]
                sums[t - a] = line if t - a not in sums else sums[t - a] + line
        return sums

    def half(weights, a, high, low):
        both = jnp.concatenate([high, low], axis=1)
        size = weights.shape[1] // 2
        middle = -(-size // 32) * 16
        lines = []
        for first, last in ((0, middle), (middle, size)):
            line = dot(weights[a, first:last, :], both) + dot(weights[a, size + first:size + last, :], both)
            lines.append(line[:, 0:cols] + line[:, cols:2 * cols])
        return jnp.concatenate(lines, axis=0)

    def widen_line(weights, a, t):
        at = t * depth
        return half(weights, a, s_high[at:at + depth, :], s_low[at:at + depth, :])

    def narrow_line(weights, a, j):
        at = j * hidden
        return half(weights, a, h_high[at:at + hidden, :], h_low[at:at + hidden, :])

    def collect(total):
        return sum(shifted(total[b * chans:(b + 1) * chans], b) for b in range(3))

    def narrow(weights, parts):
        sums = {}
        for a, outs in parts:
            lines = [i + a for i in outs]
            both = dot(weights[a], joined(h_high, hidden, lines))
            total = both[0:taps] + both[taps:2 * taps] + dot(weights[a, 0:taps, :], joined(h_low, hidden, lines))
            for n, i in enumerate(outs):
                line = total[:, n * cols:(n + 1) * cols]
                sums[i] = line if i not in sums else sums[i] + line
        return sums

    def put_hidden(j, value):
        high, low = split(value)
        h_high[j * hidden:(j + 1) * hidden, :] = high
        h_low[j * hidden:(j + 1) * hidden, :] = low

    def bend(step, j, value):
        value = value + bias[...]
        inner = jnp.tanh(gelu_scale * (value + gelu_cubic * value * value * value))
        put_hidden(j, 0.5 * value * (1.0 + inner))
        slope[step, j] = value
        bent[step, j] = inner

    def slopes_of(step):
        for j in range(rows + 2):
            value, inner = slope[step, j], bent[step, j]
            slope[step, j] = 0.5 * (1.0 + inner) + 0.5 * value * (1.0 - inner * inner) * (
                gelu_scale * (1.0 + 3.0 * gelu_cubic * value * value))

    def unbend(step, j, value):
        put_hidden(j, value * slope[step, j])

    def own_part(wide, slim, own, act):
        for i in range(rows):
            put_line(i + 2, own[i])
        for j, line in widen(wide, [(a, range(2, rows + 2)) for a in range(3)]).items():
            before[j] = line

        @pl.when(jnp.logical_not(has_slow))
        def _():
            act(1, before[1])
            for i in range(2):
                edge[i] = narrow_line(slim, 1 - i, 1)

    def convolve(wide, slim, n, own, act, finish):
        pltpu.make_async_copy(halo.at[n, 1], halo.at[n, 1], fast_recv.at[n]).wait()
        for far in range(2):
            put_line(rows + 2 + far, halo[n, 1, far])
        sums = widen(wide, [(2, (rows + 2, rows + 3)), (1, (rows + 2,))])
        for j in range(2, rows + 2):
            act(j, before[j] + sums[j] if j in sums else before[j])
        ready = [(a, [i for i in range(rows) if i + a >= 2]) for a in (2, 1, 0)]
        for i, line in narrow(slim, [part for part in ready if part[1]]).items():
            if i < 2:
                narrowed[i] = line
            else:
                finish(i, collect(line))

        @pl.when(jnp.logical_not(has_slow))
        def _():
            for i in (1, 0):
                finish(i, collect(narrowed[i] + edge[i]))

        @pl.when(has_slow)
        def _():
            to_slow(n, own, 1).wait_recv()
            put_line(0, halo[n, 0, 1])
            before[0] += widen_line(wide, 0, 0)
            to_slow(n, own, 0).wait_recv()
            put_line(1, halo[n, 0, 0])
            act(1, before[1] + widen_line(wide, 0, 1))
            act(0, before[0] + widen_line(wide, 1, 1))
            finish(1, collect(narrowed[1] + narrow_line(slim, 0, 1)))
            finish(0, collect(narrowed[0] + narrow_line(slim, 1, 1) + narrow_line(slim, 0, 0)))

    def fold(value):
        return sum(value[8 * i:8 * i + 8] for i in range(chans // 8))

    def row_weight(i):
        return jnp.where(odd == 1, lat_ref[0:1, rows - 1 - i:rows - i], lat_ref[0:1, i:i + 1])

    def apart(spread):
        square = spread * spread + smooth_width * smooth_width
        return square, lax.rsqrt(square)

    def loss_slopes(step, i):
        mine = fields[step, i]
        error = mine - target_ref[step, i]
        gradient = error * apart(error)[1]
        slopes = jnp.zeros_like(mine)
        for k in range(1, members):
            spread = mine - everyone[step, lax.rem(me_m + k, members), i]
            slopes = slopes + spread * apart(spread)[1]
        return row_weight(i) * (gradient - slopes / (members - 1))

    def band_loss(step, i):
        states = [everyone[step, m, i] for m in range(members)]
        direct = jnp.zeros_like(states[0])
        pairs = jnp.full(direct.shape, 0.5 * members * smooth_width, F32)
        for m, state in enumerate(states):
            square, inverse = apart(state - target_ref[step, i])
            direct = direct + square * inverse
            for other in states[m + 1:]:
                square, inverse = apart(state - other)
                pairs = pairs + square * inverse
        return row_weight(i) * fold(direct - pairs / (members - 1))

    for step in range(steps):
        own = x_ref if step == 0 else fields.at[step - 1]
        if step == 0:
            front_weights()
            narrow_weights()
        act = functools.partial(bend, step)
        own_part(win, wout, own, act)
        if step > 0:
            back_weights()
        if step < len(rounds):
            reached(step)
            if step + 1 < len(rounds):
                reach_out(step + 1)

        def advance(i, change):
            state = own[i] + change
            fields[step, i] = state
            everyone[step, me_m, i] = state
            if step < steps - 1:
                send_row(step + 1, fields.at[step], i)
            else:
                for k in peers:
                    to_member(step, k, i).start()

        convolve(win, wout, step, own, act, advance)
        if step < steps - 1:
            for i in range(rows):
                for k in peers:
                    to_member(step, k, i).start()

    for step in range(steps):
        slopes_of(step)
    for r in range(steps, len(rounds)):
        reached(r)
        if r + 1 < len(rounds):
            reach_out(r + 1)
    arrive(4)
    arrive(5)
    partial = jnp.zeros((8, cols), F32)
    for step in range(steps):
        for i in reversed(range(rows)):
            landed = everyone.at[step, 0:members - 1, i]
            pltpu.make_async_copy(landed, landed, other_recv.at[step, i]).wait()
            if step < steps - 1:
                loss_grad[step, i] = loss_slopes(step, i)
            else:
                grads[step, i] = loss_slopes(step, i)
                send_row(steps, grads.at[step], i)
            if step < steps - 1 or i > 0:
                partial = partial + band_loss(step, i)

    for step in range(steps - 1, -1, -1):
        n = 2 * steps - 1 - step
        own = grads.at[step]

        def retreat(i, change):
            if step > 0:
                grads[step - 1, i] = grads[step, i] + change + loss_grad[step - 1, i]
                send_row(n + 1, grads.at[step - 1], i)
            else:
                grad_ref[mirror[i]] = grads[0, i] + change

        act = functools.partial(unbend, step)
        own_part(woutb, winb, own, act)
        if step == steps - 1:
            partial = partial + band_loss(step, 0)
            parts[me_l] = jnp.sum(partial, axis=0, keepdims=True)
            for k in range(1, bands):
                pltpu.make_async_remote_copy(
                    src_ref=parts.at[me_l], dst_ref=parts.at[me_l], send_sem=part_send.at[0], recv_sem=part_recv.at[0],
                    device_id={"lat": lax.rem(me_l + k, bands)}, device_id_type=MESH).start()
        convolve(woutb, winb, n, own, act, retreat)

    sent = parts.at[0:bands - 1]
    pltpu.make_async_copy(sent, sent, part_recv.at[0]).wait()
    total = jnp.sum(parts[...], axis=0)
    count = members * steps * rows * bands * chans * cols
    loss_ref[...] = jnp.full(loss_ref.shape, jnp.sum(total) / count, F32)
    pltpu.make_async_copy(sent, sent, part_send.at[0]).wait()
    landed = everyone.at[:, 0:members - 1]
    pltpu.make_async_copy(landed, landed, other_send.at[0]).wait()
    pltpu.make_async_copy(halo.at[:, 1], halo.at[:, 1], halo_send.at[1]).wait()

    @pl.when(has_slow)
    def _():
        pltpu.make_async_copy(halo.at[:, 0], halo.at[:, 0], halo_send.at[0]).wait()


def deliver(grad_vmem, loss_vmem, grad_hbm, loss_hbm, loss_smem, sem):
    gradient = pltpu.make_async_copy(grad_vmem, grad_hbm, sem.at[0])
    loss = pltpu.make_async_copy(loss_smem, loss_hbm, sem.at[1])
    gradient.start()
    loss_smem[0, 0] = loss_vmem[0, 0]
    loss.start()
    loss.wait()
    gradient.wait()


def on_device(members, bands, initial_states, targets, lat_weight, weight_in, weight_out, hidden_bias):
    steps, rows, chans, cols = targets.shape
    hidden = weight_in.shape[0]
    taps = 3 * chans
    depth = -(-taps // 256) * 256
    deep = 3 * hidden
    vmem = pl.BlockSpec(memory_space=pltpu.VMEM)
    dma = pltpu.SemaphoreType.DMA
    gradient, loss = pl.pallas_call(
        functools.partial(kernel, members, bands),
        out_shape=(pltpu.VMEM((rows, chans, cols), F32), pltpu.VMEM((8, cols), F32)),
        in_specs=[pl.BlockSpec(memory_space=pltpu.HBM)] * 6,
        out_specs=(vmem, vmem),
        scratch_shapes=[
            pltpu.VMEM((rows, chans, cols), F32),
            pltpu.VMEM(targets.shape, F32),
            pltpu.VMEM((1, rows), F32),
            pltpu.VMEM((3 * taps, hidden), F32),
            pltpu.VMEM((chans, 3 * deep), F32),
            pltpu.VMEM((1, hidden), F32),
            dma((6,)),
            pltpu.VMEM((2 * steps, 2, 2, chans, cols), F32),
            pltpu.VMEM((steps, members, rows, chans, cols), F32),
            pltpu.VMEM((bands, 1, cols), F32),
            pltpu.VMEM((steps, rows, chans, cols), F32),
            pltpu.VMEM((steps, rows, chans, cols), F32),
            pltpu.VMEM((3, 2 * hidden, depth), BF16),
            pltpu.VMEM((3, 2 * taps, hidden), BF16),
            pltpu.VMEM((3, 2 * taps, hidden), BF16),
            pltpu.VMEM((3, 2 * hidden, depth), BF16),
            pltpu.VMEM((depth, hidden), F32),
            pltpu.VMEM(((rows + 4) * depth, cols), BF16),
            pltpu.VMEM(((rows + 4) * depth, cols), BF16),
            pltpu.VMEM(((rows + 2) * hidden, cols), BF16),
            pltpu.VMEM(((rows + 2) * hidden, cols), BF16),
            pltpu.VMEM((rows + 2, hidden, cols), F32),
            pltpu.VMEM((steps, rows + 2, hidden, cols), F32),
            pltpu.VMEM((steps, rows + 2, hidden, cols), F32),
            pltpu.VMEM((2, taps, cols), F32),
            pltpu.VMEM((2, taps, cols), F32),
            pltpu.VMEM((steps - 1, rows, chans, cols), F32),
            pltpu.VMEM((hidden, cols), F32),
            dma((2,)), dma((2 * steps, 2)), dma((2 * steps,)),
            dma((1,)), dma((steps, rows)),
            dma((1,)), dma((1,)),
            pltpu.SemaphoreType.REGULAR((max(1, (bands - 2).bit_length()),)),
        ],
        compiler_params=pltpu.CompilerParams(collective_id=0, has_side_effects=True, vmem_limit_bytes=24 * 2**20),
    )(
        *(pltpu.with_memory_space_constraint(value, pltpu.HBM) for value in (
            initial_states.reshape(rows, chans, cols), targets, lat_weight.reshape(1, rows),
            weight_in.T, weight_out, hidden_bias.reshape(1, hidden)))
    )
    anywhere = pl.BlockSpec(memory_space=pl.ANY)
    gradient, loss = pl.pallas_call(
        deliver,
        out_shape=(jax.ShapeDtypeStruct((rows, chans, cols), F32), jax.ShapeDtypeStruct((1, 1), F32)),
        in_specs=[vmem, vmem],
        out_specs=(anywhere, anywhere),
        scratch_shapes=[pltpu.SMEM((1, 1), F32), dma((2,))],
    )(*(pltpu.with_memory_space_constraint(value, pltpu.VMEM) for value in (gradient, loss)))
    return gradient.reshape(initial_states.shape), loss.reshape(())


def solution(mesh):
    placed = (P("member", "lat", None, None), P(None, "lat", None, None), P("lat"), P(), P(), P())
    return jax.shard_map(
        functools.partial(on_device, mesh.shape["member"], mesh.shape["lat"]),
        mesh=mesh,
        in_specs=placed,
        out_specs=(P("member", "lat", None, None), P()),
        check_vma=False,
    )
```

```python
import functools

import jax
import jax.numpy as jnp
from jax import lax
from jax.experimental import pallas as pl
from jax.experimental.pallas import tpu as pltpu
from jax.sharding import PartitionSpec as P

smooth_width = 0.1
gelu_scale = 0.7978845608028654
gelu_cubic = 0.044715
MESH = pl.DeviceIdType.MESH
F32 = jnp.float32
BF16 = jnp.bfloat16


def split(value):
    high = value.astype(BF16)
    low = (value - high.astype(F32)).astype(BF16)
    return high, low


def shifted(value, tap):
    if tap == 1:
        return value
    columns = value.shape[-1]
    lane = lax.broadcasted_iota(jnp.int32, value.shape, 1)
    if tap == 0:
        return jnp.where(lane == 0, 0.0, pltpu.roll(value, 1, 1))
    return jnp.where(lane == columns - 1, 0.0, pltpu.roll(value, columns - 1, 1))


def dot(left, right):
    return jnp.dot(left, right, preferred_element_type=F32)


def kernel(
    members, bands,
    x_hbm, target_hbm, lat_hbm, w_in_hbm, w_out_hbm, bias_hbm,
    grad_ref, loss_ref,
    x_ref, target_ref, lat_ref, w_in_ref, w_out_ref, bias_ref, fetch_sem,
    halo, everyone, parts, fields, grads,
    win, winb, wout, woutb, tall, s_high, s_low, h_high, h_low, before, slope, bent, narrowed, edge, loss_grad, bias,
    halo_send, slow_recv, fast_recv, other_send, other_recv, part_send, part_recv, reach,
):
    steps, rows, chans, cols = target_ref.shape
    hidden = w_in_ref.shape[1]
    taps = 3 * chans
    depth = win.shape[2]
    me_m = lax.axis_index("member")
    me_l = lax.axis_index("lat")
    odd = lax.rem(me_l, 2)
    slow = me_l - 1 + 2 * odd
    fast = me_l + 1 - 2 * odd
    has_slow = jnp.logical_and(slow >= 0, slow < bands)
    slow = jnp.clip(slow, 0, bands - 1)

    def mirrored(n, last):
        return n + odd * (last - 2 * n)

    def fetch(n, copies):
        return [pltpu.make_async_copy(source, target, fetch_sem.at[n]) for source, target in copies]

    mirror = [mirrored(i, rows - 1) for i in range(rows)]
    fetches = [
        fetch(0, [(x_hbm.at[mirror[i]], x_ref.at[i]) for i in range(rows)]),
        fetch(1, [(w_in_hbm, w_in_ref)]),
        fetch(2, [(bias_hbm, bias_ref)]),
        fetch(3, [(w_out_hbm, w_out_ref)]),
        fetch(4, [(target_hbm.at[:, mirror[i]], target_ref.at[:, i]) for i in range(rows)]),
        fetch(5, [(lat_hbm, lat_ref)]),
    ]
    arrivals = [x_ref, w_in_ref, bias_ref, w_out_ref, target_ref, lat_ref]

    def arrive(n):
        pltpu.make_async_copy(arrivals[n], arrivals[n], fetch_sem.at[n]).wait()

    for copy in fetches[0]:
        copy.start()
    barrier = pltpu.get_barrier_semaphore()
    for k in range(1, members):
        pl.semaphore_signal(barrier, inc=1, device_id={"member": lax.rem(me_m + k, members)}, device_id_type=MESH)
    pl.semaphore_signal(barrier, inc=1, device_id={"lat": fast}, device_id_type=MESH)

    @pl.when(has_slow)
    def _():
        pl.semaphore_signal(barrier, inc=1, device_id={"lat": slow}, device_id_type=MESH)

    for copies in fetches[1:]:
        for copy in copies:
            copy.start()

    def to_slow(n, source, far):
        return pltpu.make_async_remote_copy(
            src_ref=source.at[far], dst_ref=halo.at[n, 0, far],
            send_sem=halo_send.at[0], recv_sem=slow_recv.at[n, far],
            device_id={"lat": slow}, device_id_type=MESH)

    def to_fast(n, source, far):
        return pltpu.make_async_remote_copy(
            src_ref=source.at[rows - 1 - far], dst_ref=halo.at[n, 1, far],
            send_sem=halo_send.at[1], recv_sem=fast_recv.at[n],
            device_id={"lat": fast}, device_id_type=MESH)

    def send_row(n, source, i):
        if i < 2:
            @pl.when(has_slow)
            def _():
                to_slow(n, source, i).start()

        if rows - 1 - i < 2:
            to_fast(n, source, rows - 1 - i).start()

    def peer(k):
        if members & (members - 1):
            return lax.rem(me_m + k, members)
        result, bit = 0, 1
        while bit < members:
            mine = lax.rem(me_m // bit, 2)
            result = result + bit * (1 - mine if k & bit else mine)
            bit *= 2
        return result

    peers = sorted(range(1, members), key=lambda k: -bin(k).count("1"))

    def to_member(step, k, i):
        return pltpu.make_async_remote_copy(
            src_ref=everyone.at[step, me_m, i], dst_ref=everyone.at[step, me_m, i],
            send_sem=other_send.at[0], recv_sem=other_recv.at[step, i],
            device_id={"member": peer(k)}, device_id_type=MESH)

    rounds = [1]
    while 2 * rounds[-1] < bands - 1:
        rounds.append(2 * rounds[-1])

    def reach_out(r):
        for far in (me_l - rounds[r], me_l + rounds[r]):
            @pl.when(jnp.logical_and(far >= 0, far < bands))
            def _():
                pl.semaphore_signal(
                    reach.at[r], inc=1, device_id={"lat": jnp.clip(far, 0, bands - 1)}, device_id_type=MESH)

    def reached(r):
        below = (me_l >= rounds[r]).astype(jnp.int32)
        above = (me_l + rounds[r] < bands).astype(jnp.int32)
        pl.semaphore_wait(reach.at[r], below + above)

    arrive(0)
    pl.semaphore_wait(barrier, members + has_slow.astype(jnp.int32))
    for i in reversed(range(rows)):
        send_row(0, x_ref, i)
    reach_out(0)

    def put_wide(target, a, block):
        tall[0:taps, :] = block
        high, low = split(tall[...].T)
        target[a, 0:hidden] = high
        target[a, hidden:2 * hidden] = low

    def tap_rows(a):
        return pl.ds(pl.multiple_of(mirrored(a, 2) * taps, 8), taps)

    def tap_block(a, b, size, unit):
        return pl.ds(pl.multiple_of((3 * mirrored(a, 2) + b) * size, unit), size)

    def front_weights():
        arrive(1)
        arrive(2)
        tall[taps:, :] = jnp.zeros((depth - taps, hidden), F32)
        for a in range(3):
            put_wide(win, a, w_in_ref[tap_rows(a), :])
        bias[...] = jnp.broadcast_to(bias_ref[...], (cols, hidden)).T
        for t in range(rows + 4):
            s_high[t * depth + taps:(t + 1) * depth, :] = jnp.zeros((depth - taps, cols), BF16)
            s_low[t * depth + taps:(t + 1) * depth, :] = jnp.zeros((depth - taps, cols), BF16)

    def narrow_weights():
        arrive(3)
        for a in range(3):
            for b in range(3):
                high, low = split(w_out_ref[:, tap_block(a, b, hidden, 128)])
                wout[a, b * chans:(b + 1) * chans, :] = high
                wout[a, taps + b * chans:taps + (b + 1) * chans, :] = low

    def back_weights():
        for a in range(3):
            for b in range(3):
                high, low = split(w_in_ref[tap_block(2 - a, 2 - b, chans, 8), :])
                winb[a, b * chans:(b + 1) * chans, :] = high
                winb[a, taps + b * chans:taps + (b + 1) * chans, :] = low
        for a in range(3):
            put_wide(woutb, a, jnp.concatenate(
                [w_out_ref[:, tap_block(2 - a, 2 - b, hidden, 128)] for b in range(3)], axis=0))

    def put_line(t, line):
        for b in range(3):
            high, low = split(shifted(line, b))
            at = t * depth + b * chans
            s_high[at:at + chans, :] = high
            s_low[at:at + chans, :] = low

    def joined(ref, size, lines):
        return jnp.concatenate([ref[t * size:(t + 1) * size, :] for t in lines], axis=1)

    def widen(weights, parts):
        sums = {}
        for a, lines in parts:
            high = joined(s_high, depth, lines)
            low = joined(s_low, depth, lines)
            both = dot(weights[a], high)
            total = both[0:hidden] + both[hidden:2 * hidden] + dot(weights[a, 0:hidden, :], low)
            for n, t in enumerate(lines):
                line = total[:, n * cols:(n + 1) * cols]
                sums[t - a] = line if t - a not in sums else sums[t - a] + line
        return sums

    def half(weights, terms, pieces=2):
        size = weights.shape[1] // 2
        edges = [0] + [-(-size * p // (16 * pieces)) * 16 for p in range(1, pieces)] + [size]
        lines = []
        for first, last in zip(edges, edges[1:]):
            line = sum(
                dot(weights[a, at + first:at + last, :], both) for a, both in terms for at in (0, size))
            lines.append(line[:, 0:cols] + line[:, cols:2 * cols])
        return jnp.concatenate(lines, axis=0)

    def beside(high, low, size, t):
        return jnp.concatenate([high[t * size:(t + 1) * size, :], low[t * size:(t + 1) * size, :]], axis=1)

    def widen_line(weights, a, t, pieces=2):
        return half(weights, [(a, beside(s_high, s_low, depth, t))], pieces)

    def narrow_line(weights, *taps_of):
        return half(weights, [(a, beside(h_high, h_low, hidden, j)) for a, j in taps_of])

    def collect(total):
        return sum(shifted(total[b * chans:(b + 1) * chans], b) for b in range(3))

    def narrow(weights, parts):
        sums = {}
        for a, outs in parts:
            lines = [i + a for i in outs]
            both = dot(weights[a], joined(h_high, hidden, lines))
            total = both[0:taps] + both[taps:2 * taps] + dot(weights[a, 0:taps, :], joined(h_low, hidden, lines))
            for n, i in enumerate(outs):
                line = total[:, n * cols:(n + 1) * cols]
                sums[i] = line if i not in sums else sums[i] + line
        return sums

    def put_hidden(j, value):
        high, low = split(value)
        h_high[j * hidden:(j + 1) * hidden, :] = high
        h_low[j * hidden:(j + 1) * hidden, :] = low

    def bend(step, j, value):
        value = value + bias[...]
        inner = jnp.tanh(gelu_scale * (value + gelu_cubic * value * value * value))
        put_hidden(j, 0.5 * value * (1.0 + inner))
        slope[step, j] = value
        bent[step, j] = inner

    def slopes_of(step):
        for j in range(rows + 2):
            value, inner = slope[step, j], bent[step, j]
            slope[step, j] = 0.5 * (1.0 + inner) + 0.5 * value * (1.0 - inner * inner) * (
                gelu_scale * (1.0 + 3.0 * gelu_cubic * value * value))

    def unbend(step, j, value):
        put_hidden(j, value * slope[step, j])

    def own_part(wide, slim, own, act):
        for i in range(rows):
            put_line(i + 2, own[i])
        for j, line in widen(wide, [(a, range(2, rows + 2)) for a in range(3)]).items():
            before[j] = line

        @pl.when(jnp.logical_not(has_slow))
        def _():
            act(1, before[1])
            for i in range(2):
                edge[i] = narrow_line(slim, (1 - i, 1))

    def convolve(wide, slim, n, own, act, finish):
        pltpu.make_async_copy(halo.at[n, 1], halo.at[n, 1], fast_recv.at[n]).wait()
        for far in range(2):
            put_line(rows + 2 + far, halo[n, 1, far])
        sums = widen(wide, [(2, (rows + 2, rows + 3)), (1, (rows + 2,))])
        for j in range(2, rows + 2):
            act(j, before[j] + sums[j] if j in sums else before[j])
        ready = [(a, [i for i in range(rows) if i + a >= 2]) for a in (2, 1, 0)]
        for i, line in narrow(slim, [part for part in ready if part[1]]).items():
            if i < 2:
                narrowed[i] = line
            else:
                finish(i, collect(line))

        @pl.when(jnp.logical_not(has_slow))
        def _():
            for i in (1, 0):
                finish(i, collect(narrowed[i] + edge[i]))

        @pl.when(has_slow)
        def _():
            to_slow(n, own, 1).wait_recv()
            put_line(0, halo[n, 0, 1])
            before[0] += widen_line(wide, 0, 0)
            to_slow(n, own, 0).wait_recv()
            put_line(1, halo[n, 0, 0])
            act(1, before[1] + widen_line(wide, 0, 1))
            act(0, before[0] + widen_line(wide, 1, 1))
            finish(1, collect(narrowed[1] + narrow_line(slim, (0, 1))))
            finish(0, collect(narrowed[0] + narrow_line(slim, (1, 1), (0, 0))))

    def fold(value):
        return sum(value[8 * i:8 * i + 8] for i in range(chans // 8))

    def row_weight(i):
        return jnp.where(odd == 1, lat_ref[0:1, rows - 1 - i:rows - i], lat_ref[0:1, i:i + 1])

    def apart(spread):
        square = spread * spread + smooth_width * smooth_width
        return square, lax.rsqrt(square)

    def loss_slopes(step, i):
        mine = fields[step, i]
        error = mine - target_ref[step, i]
        gradient = error * apart(error)[1]
        slopes = jnp.zeros_like(mine)
        for k in range(1, members):
            spread = mine - everyone[step, lax.rem(me_m + k, members), i]
            slopes = slopes + spread * apart(spread)[1]
        return row_weight(i) * (gradient - slopes / (members - 1))

    def band_loss(step, i):
        states = [everyone[step, m, i] for m in range(members)]
        direct = jnp.zeros_like(states[0])
        pairs = jnp.full(direct.shape, 0.5 * members * smooth_width, F32)
        for m, state in enumerate(states):
            square, inverse = apart(state - target_ref[step, i])
            direct = direct + square * inverse
            for other in states[m + 1:]:
                square, inverse = apart(state - other)
                pairs = pairs + square * inverse
        return row_weight(i) * fold(direct - pairs / (members - 1))

    for step in range(steps):
        own = x_ref if step == 0 else fields.at[step - 1]
        if step == 0:
            front_weights()
            narrow_weights()
        act = functools.partial(bend, step)
        own_part(win, wout, own, act)
        if step < len(rounds):
            reached(step)
            if step + 1 < len(rounds):
                reach_out(step + 1)

        def advance(i, change):
            state = own[i] + change
            fields[step, i] = state
            everyone[step, me_m, i] = state
            if step < steps - 1:
                send_row(step + 1, fields.at[step], i)
            else:
                for k in peers:
                    to_member(step, k, i).start()

        convolve(win, wout, step, own, act, advance)
        if step < steps - 1:
            for i in range(rows):
                for k in peers:
                    to_member(step, k, i).start()

    back_weights()
    for step in range(steps):
        slopes_of(step)
    for r in range(steps, len(rounds)):
        reached(r)
        if r + 1 < len(rounds):
            reach_out(r + 1)
    arrive(4)
    arrive(5)
    partial = jnp.zeros((8, cols), F32)
    for step in range(steps):
        for i in reversed(range(rows)):
            landed = everyone.at[step, 0:members - 1, i]
            pltpu.make_async_copy(landed, landed, other_recv.at[step, i]).wait()
            if step < steps - 1:
                loss_grad[step, i] = loss_slopes(step, i)
            else:
                grads[step, i] = loss_slopes(step, i)
                send_row(steps, grads.at[step], i)
            if step < steps - 1 or i > 0:
                partial = partial + band_loss(step, i)

    for step in range(steps - 1, -1, -1):
        n = 2 * steps - 1 - step
        own = grads.at[step]

        def retreat(i, change):
            if step > 0:
                grads[step - 1, i] = grads[step, i] + change + loss_grad[step - 1, i]
                send_row(n + 1, grads.at[step - 1], i)
            else:
                grad_ref[mirror[i]] = grads[0, i] + change

        act = functools.partial(unbend, step)
        own_part(woutb, winb, own, act)
        if step == steps - 1:
            partial = partial + band_loss(step, 0)
            parts[me_l] = jnp.sum(partial, axis=0, keepdims=True)
            for k in range(1, bands):
                pltpu.make_async_remote_copy(
                    src_ref=parts.at[me_l], dst_ref=parts.at[me_l], send_sem=part_send.at[0], recv_sem=part_recv.at[0],
                    device_id={"lat": lax.rem(me_l + k, bands)}, device_id_type=MESH).start()
        convolve(woutb, winb, n, own, act, retreat)

    sent = parts.at[0:bands - 1]
    pltpu.make_async_copy(sent, sent, part_recv.at[0]).wait()
    total = jnp.sum(parts[...], axis=0)
    count = members * steps * rows * bands * chans * cols
    loss_ref[...] = jnp.full(loss_ref.shape, jnp.sum(total) / count, F32)
    pltpu.make_async_copy(sent, sent, part_send.at[0]).wait()
    landed = everyone.at[:, 0:members - 1]
    pltpu.make_async_copy(landed, landed, other_send.at[0]).wait()
    pltpu.make_async_copy(halo.at[:, 1], halo.at[:, 1], halo_send.at[1]).wait()

    @pl.when(has_slow)
    def _():
        pltpu.make_async_copy(halo.at[:, 0], halo.at[:, 0], halo_send.at[0]).wait()


def deliver(grad_vmem, loss_vmem, grad_hbm, loss_hbm, loss_smem, sem):
    gradient = pltpu.make_async_copy(grad_vmem, grad_hbm, sem.at[0])
    loss = pltpu.make_async_copy(loss_smem, loss_hbm, sem.at[1])
    gradient.start()
    loss_smem[0, 0] = loss_vmem[0, 0]
    loss.start()
    loss.wait()
    gradient.wait()


def on_device(members, bands, initial_states, targets, lat_weight, weight_in, weight_out, hidden_bias):
    steps, rows, chans, cols = targets.shape
    hidden = weight_in.shape[0]
    taps = 3 * chans
    depth = -(-taps // 256) * 256
    deep = 3 * hidden
    vmem = pl.BlockSpec(memory_space=pltpu.VMEM)
    dma = pltpu.SemaphoreType.DMA
    gradient, loss = pl.pallas_call(
        functools.partial(kernel, members, bands),
        out_shape=(pltpu.VMEM((rows, chans, cols), F32), pltpu.VMEM((8, cols), F32)),
        in_specs=[pl.BlockSpec(memory_space=pltpu.HBM)] * 6,
        out_specs=(vmem, vmem),
        scratch_shapes=[
            pltpu.VMEM((rows, chans, cols), F32),
            pltpu.VMEM(targets.shape, F32),
            pltpu.VMEM((1, rows), F32),
            pltpu.VMEM((3 * taps, hidden), F32),
            pltpu.VMEM((chans, 3 * deep), F32),
            pltpu.VMEM((1, hidden), F32),
            dma((6,)),
            pltpu.VMEM((2 * steps, 2, 2, chans, cols), F32),
            pltpu.VMEM((steps, members, rows, chans, cols), F32),
            pltpu.VMEM((bands, 1, cols), F32),
            pltpu.VMEM((steps, rows, chans, cols), F32),
            pltpu.VMEM((steps, rows, chans, cols), F32),
            pltpu.VMEM((3, 2 * hidden, depth), BF16),
            pltpu.VMEM((3, 2 * taps, hidden), BF16),
            pltpu.VMEM((3, 2 * taps, hidden), BF16),
            pltpu.VMEM((3, 2 * hidden, depth), BF16),
            pltpu.VMEM((depth, hidden), F32),
            pltpu.VMEM(((rows + 4) * depth, cols), BF16),
            pltpu.VMEM(((rows + 4) * depth, cols), BF16),
            pltpu.VMEM(((rows + 2) * hidden, cols), BF16),
            pltpu.VMEM(((rows + 2) * hidden, cols), BF16),
            pltpu.VMEM((rows + 2, hidden, cols), F32),
            pltpu.VMEM((steps, rows + 2, hidden, cols), F32),
            pltpu.VMEM((steps, rows + 2, hidden, cols), F32),
            pltpu.VMEM((2, taps, cols), F32),
            pltpu.VMEM((2, taps, cols), F32),
            pltpu.VMEM((steps - 1, rows, chans, cols), F32),
            pltpu.VMEM((hidden, cols), F32),
            dma((2,)), dma((2 * steps, 2)), dma((2 * steps,)),
            dma((1,)), dma((steps, rows)),
            dma((1,)), dma((1,)),
            pltpu.SemaphoreType.REGULAR((max(1, (bands - 2).bit_length()),)),
        ],
        compiler_params=pltpu.CompilerParams(collective_id=0, has_side_effects=True, vmem_limit_bytes=24 * 2**20),
    )(
        *(pltpu.with_memory_space_constraint(value, pltpu.HBM) for value in (
            initial_states.reshape(rows, chans, cols), targets, lat_weight.reshape(1, rows),
            weight_in.T, weight_out, hidden_bias.reshape(1, hidden)))
    )
    anywhere = pl.BlockSpec(memory_space=pl.ANY)
    gradient, loss = pl.pallas_call(
        deliver,
        out_shape=(jax.ShapeDtypeStruct((rows, chans, cols), F32), jax.ShapeDtypeStruct((1, 1), F32)),
        in_specs=[vmem, vmem],
        out_specs=(anywhere, anywhere),
        scratch_shapes=[pltpu.SMEM((1, 1), F32), dma((2,))],
    )(*(pltpu.with_memory_space_constraint(value, pltpu.VMEM) for value in (gradient, loss)))
    return gradient.reshape(initial_states.shape), loss.reshape(())


def solution(mesh):
    placed = (P("member", "lat", None, None), P(None, "lat", None, None), P("lat"), P(), P(), P())
    return jax.shard_map(
        functools.partial(on_device, mesh.shape["member"], mesh.shape["lat"]),
        mesh=mesh,
        in_specs=placed,
        out_specs=(P("member", "lat", None, None), P()),
        check_vma=False,
    )
```

```python
import functools

import jax
import jax.numpy as jnp
from jax import lax
from jax.experimental import pallas as pl
from jax.experimental.pallas import tpu as pltpu
from jax.sharding import PartitionSpec as P

smooth_width = 0.1
gelu_scale = 0.7978845608028654
gelu_cubic = 0.044715
MESH = pl.DeviceIdType.MESH
F32 = jnp.float32
BF16 = jnp.bfloat16


def split(value):
    high = value.astype(BF16)
    low = (value - high.astype(F32)).astype(BF16)
    return high, low


def shifted(value, tap):
    if tap == 1:
        return value
    columns = value.shape[-1]
    lane = lax.broadcasted_iota(jnp.int32, value.shape, 1)
    if tap == 0:
        return jnp.where(lane == 0, 0.0, pltpu.roll(value, 1, 1))
    return jnp.where(lane == columns - 1, 0.0, pltpu.roll(value, columns - 1, 1))


def dot(left, right):
    return jnp.dot(left, right, preferred_element_type=F32)


def kernel(
    members, bands,
    x_hbm, target_hbm, lat_hbm, w_in_hbm, w_out_hbm, bias_hbm,
    grad_ref, loss_ref,
    x_ref, target_ref, lat_ref, w_in_ref, w_out_ref, bias_ref, fetch_sem,
    halo, everyone, parts, fields, grads,
    win, winb, wout, woutb, tall, s_high, s_low, h_high, h_low, before, slope, bent, narrowed, edge, loss_grad, bias,
    halo_send, slow_recv, fast_recv, other_send, other_recv, part_send, part_recv, reach,
):
    steps, rows, chans, cols = target_ref.shape
    hidden = w_in_ref.shape[1]
    taps = 3 * chans
    depth = win.shape[2]
    me_m = lax.axis_index("member")
    me_l = lax.axis_index("lat")
    odd = lax.rem(me_l, 2)
    slow = me_l - 1 + 2 * odd
    fast = me_l + 1 - 2 * odd
    has_slow = jnp.logical_and(slow >= 0, slow < bands)
    slow = jnp.clip(slow, 0, bands - 1)

    def mirrored(n, last):
        return n + odd * (last - 2 * n)

    def fetch(n, copies):
        return [pltpu.make_async_copy(source, target, fetch_sem.at[n]) for source, target in copies]

    mirror = [mirrored(i, rows - 1) for i in range(rows)]
    fetches = [
        fetch(0, [(x_hbm.at[mirror[i]], x_ref.at[i]) for i in range(rows)]),
        fetch(1, [(w_in_hbm, w_in_ref)]),
        fetch(2, [(bias_hbm, bias_ref)]),
        fetch(3, [(w_out_hbm, w_out_ref)]),
        fetch(4, [(target_hbm.at[:, mirror[i]], target_ref.at[:, i]) for i in range(rows)]),
        fetch(5, [(lat_hbm, lat_ref)]),
    ]
    arrivals = [x_ref, w_in_ref, bias_ref, w_out_ref, target_ref, lat_ref]

    def arrive(n):
        pltpu.make_async_copy(arrivals[n], arrivals[n], fetch_sem.at[n]).wait()

    for copy in fetches[0]:
        copy.start()
    barrier = pltpu.get_barrier_semaphore()
    for k in range(1, members):
        pl.semaphore_signal(barrier, inc=1, device_id={"member": lax.rem(me_m + k, members)}, device_id_type=MESH)
    pl.semaphore_signal(barrier, inc=1, device_id={"lat": fast}, device_id_type=MESH)

    @pl.when(has_slow)
    def _():
        pl.semaphore_signal(barrier, inc=1, device_id={"lat": slow}, device_id_type=MESH)

    for copies in fetches[1:]:
        for copy in copies:
            copy.start()

    def to_slow(n, source, far):
        return pltpu.make_async_remote_copy(
            src_ref=source.at[far], dst_ref=halo.at[n, 0, far],
            send_sem=halo_send.at[0], recv_sem=slow_recv.at[n, far],
            device_id={"lat": slow}, device_id_type=MESH)

    def to_fast(n, source, far):
        return pltpu.make_async_remote_copy(
            src_ref=source.at[rows - 1 - far], dst_ref=halo.at[n, 1, far],
            send_sem=halo_send.at[1], recv_sem=fast_recv.at[n],
            device_id={"lat": fast}, device_id_type=MESH)

    def send_row(n, source, i):
        if i < 2:
            @pl.when(has_slow)
            def _():
                to_slow(n, source, i).start()

        if rows - 1 - i < 2:
            to_fast(n, source, rows - 1 - i).start()

    def peer(k):
        if members & (members - 1):
            return lax.rem(me_m + k, members)
        result, bit = 0, 1
        while bit < members:
            mine = lax.rem(me_m // bit, 2)
            result = result + bit * (1 - mine if k & bit else mine)
            bit *= 2
        return result

    peers = sorted(range(1, members), key=lambda k: -bin(k).count("1"))

    def to_member(step, k, i):
        return pltpu.make_async_remote_copy(
            src_ref=everyone.at[step, me_m, i], dst_ref=everyone.at[step, me_m, i],
            send_sem=other_send.at[0], recv_sem=other_recv.at[step, i],
            device_id={"member": peer(k)}, device_id_type=MESH)

    rounds = [1]
    while 2 * rounds[-1] < bands - 1:
        rounds.append(2 * rounds[-1])

    def reach_out(r):
        for far in (me_l - rounds[r], me_l + rounds[r]):
            @pl.when(jnp.logical_and(far >= 0, far < bands))
            def _():
                pl.semaphore_signal(
                    reach.at[r], inc=1, device_id={"lat": jnp.clip(far, 0, bands - 1)}, device_id_type=MESH)

    def reached(r):
        below = (me_l >= rounds[r]).astype(jnp.int32)
        above = (me_l + rounds[r] < bands).astype(jnp.int32)
        pl.semaphore_wait(reach.at[r], below + above)

    arrive(0)
    pl.semaphore_wait(barrier, members + has_slow.astype(jnp.int32))
    for i in reversed(range(rows)):
        send_row(0, x_ref, i)
    reach_out(0)

    def put_wide(target, a, block):
        tall[0:taps, :] = block
        high, low = split(tall[...].T)
        target[a, 0:hidden] = high
        target[a, hidden:2 * hidden] = low

    def tap_rows(a):
        return pl.ds(pl.multiple_of(mirrored(a, 2) * taps, 8), taps)

    def tap_block(a, b, size, unit):
        return pl.ds(pl.multiple_of((3 * mirrored(a, 2) + b) * size, unit), size)

    def front_weights():
        arrive(1)
        arrive(2)
        tall[taps:, :] = jnp.zeros((depth - taps, hidden), F32)
        for a in range(3):
            put_wide(win, a, w_in_ref[tap_rows(a), :])
        bias[...] = jnp.broadcast_to(bias_ref[...], (cols, hidden)).T
        for t in range(rows + 4):
            s_high[t * depth + taps:(t + 1) * depth, :] = jnp.zeros((depth - taps, cols), BF16)
            s_low[t * depth + taps:(t + 1) * depth, :] = jnp.zeros((depth - taps, cols), BF16)

    def narrow_weights():
        arrive(3)
        for a in range(3):
            for b in range(3):
                high, low = split(w_out_ref[:, tap_block(a, b, hidden, 128)])
                wout[a, b * chans:(b + 1) * chans, :] = high
                wout[a, taps + b * chans:taps + (b + 1) * chans, :] = low

    def back_weights():
        for a in range(3):
            for b in range(3):
                high, low = split(w_in_ref[tap_block(2 - a, 2 - b, chans, 8), :])
                winb[a, b * chans:(b + 1) * chans, :] = high
                winb[a, taps + b * chans:taps + (b + 1) * chans, :] = low
        for a in range(3):
            put_wide(woutb, a, jnp.concatenate(
                [w_out_ref[:, tap_block(2 - a, 2 - b, hidden, 128)] for b in range(3)], axis=0))

    def put_line(t, line):
        for b in range(3):
            high, low = split(shifted(line, b))
            at = t * depth + b * chans
            s_high[at:at + chans, :] = high
            s_low[at:at + chans, :] = low

    def joined(ref, size, lines):
        return jnp.concatenate([ref[t * size:(t + 1) * size, :] for t in lines], axis=1)

    def widen(weights, parts):
        sums = {}
        for a, lines in parts:
            high = joined(s_high, depth, lines)
            low = joined(s_low, depth, lines)
            total = jnp.concatenate([
                dot(weights[a, at:at + hidden // 2, :], high) + dot(weights[a, hidden + at:hidden + at + hidden // 2, :], high)
                + dot(weights[a, at:at + hidden // 2, :], low) for at in (0, hidden // 2)], axis=0)
            for n, t in enumerate(lines):
                line = total[:, n * cols:(n + 1) * cols]
                sums[t - a] = line if t - a not in sums else sums[t - a] + line
        return sums

    def half(weights, terms, pieces=2):
        size = weights.shape[1] // 2
        edges = [0] + [-(-size * p // (16 * pieces)) * 16 for p in range(1, pieces)] + [size]
        lines = []
        for first, last in zip(edges, edges[1:]):
            line = sum(
                dot(weights[a, at + first:at + last, :], both) for a, both in terms for at in (0, size))
            lines.append(line[:, 0:cols] + line[:, cols:2 * cols])
        return jnp.concatenate(lines, axis=0)

    def beside(high, low, size, t):
        return jnp.concatenate([high[t * size:(t + 1) * size, :], low[t * size:(t + 1) * size, :]], axis=1)

    def widen_line(weights, a, t, pieces=2):
        return half(weights, [(a, beside(s_high, s_low, depth, t))], pieces)

    def narrow_line(weights, *taps_of):
        return half(weights, [(a, beside(h_high, h_low, hidden, j)) for a, j in taps_of])

    def collect(total):
        return sum(shifted(total[b * chans:(b + 1) * chans], b) for b in range(3))

    def narrow(weights, parts):
        sums = {}
        for a, outs in parts:
            lines = [i + a for i in outs]
            both = dot(weights[a], joined(h_high, hidden, lines))
            total = both[0:taps] + both[taps:2 * taps] + dot(weights[a, 0:taps, :], joined(h_low, hidden, lines))
            for n, i in enumerate(outs):
                line = total[:, n * cols:(n + 1) * cols]
                sums[i] = line if i not in sums else sums[i] + line
        return sums

    def put_hidden(j, value):
        high, low = split(value)
        h_high[j * hidden:(j + 1) * hidden, :] = high
        h_low[j * hidden:(j + 1) * hidden, :] = low

    def bend(step, j, value):
        value = value + bias[...]
        inner = jnp.tanh(gelu_scale * (value + gelu_cubic * value * value * value))
        put_hidden(j, 0.5 * value * (1.0 + inner))
        slope[step, j] = value
        bent[step, j] = inner

    def slopes_of(step):
        for j in range(rows + 2):
            value, inner = slope[step, j], bent[step, j]
            slope[step, j] = 0.5 * (1.0 + inner) + 0.5 * value * (1.0 - inner * inner) * (
                gelu_scale * (1.0 + 3.0 * gelu_cubic * value * value))

    def unbend(step, j, value):
        put_hidden(j, value * slope[step, j])

    def own_part(wide, slim, own, act):
        for i in range(rows):
            put_line(i + 2, own[i])
        for j, line in widen(wide, [(a, range(2, rows + 2)) for a in range(3)]).items():
            before[j] = line

        @pl.when(jnp.logical_not(has_slow))
        def _():
            act(1, before[1])
            for i in range(2):
                edge[i] = narrow_line(slim, (1 - i, 1))

    def convolve(wide, slim, n, own, act, finish):
        pltpu.make_async_copy(halo.at[n, 1], halo.at[n, 1], fast_recv.at[n]).wait()
        for far in range(2):
            put_line(rows + 2 + far, halo[n, 1, far])
        sums = widen(wide, [(2, (rows + 2, rows + 3))])
        sums[rows + 1] = sums[rows + 1] + widen_line(wide, 1, rows + 2)
        for j in range(2, rows + 2):
            act(j, before[j] + sums[j] if j in sums else before[j])
        ready = [(a, [i for i in range(rows) if i + a >= 2]) for a in (2, 1, 0)]
        outs = narrow(slim, [part for part in ready if len(part[1]) > 1])
        for a, alone in ready:
            if len(alone) == 1:
                outs[alone[0]] = outs[alone[0]] + narrow_line(slim, (a, alone[0] + a))
        for i, line in outs.items():
            if i < 2:
                narrowed[i] = line
            else:
                finish(i, collect(line))

        @pl.when(jnp.logical_not(has_slow))
        def _():
            for i in (1, 0):
                finish(i, collect(narrowed[i] + edge[i]))

        @pl.when(has_slow)
        def _():
            to_slow(n, own, 1).wait_recv()
            put_line(0, halo[n, 0, 1])
            before[0] += widen_line(wide, 0, 0)
            to_slow(n, own, 0).wait_recv()
            put_line(1, halo[n, 0, 0])
            line1 = before[1] + widen_line(wide, 0, 1)
            line0 = before[0] + widen_line(wide, 1, 1)
            act(1, line1)
            out1 = collect(narrowed[1] + narrow_line(slim, (0, 1)))
            act(0, line0)
            finish(1, out1)
            finish(0, collect(narrowed[0] + narrow_line(slim, (1, 1), (0, 0))))

    def fold(value):
        return sum(value[8 * i:8 * i + 8] for i in range(chans // 8))

    def row_weight(i):
        return jnp.where(odd == 1, lat_ref[0:1, rows - 1 - i:rows - i], lat_ref[0:1, i:i + 1])

    def apart(spread):
        square = spread * spread + smooth_width * smooth_width
        return square, lax.rsqrt(square)

    def loss_slopes(step, i):
        mine = fields[step, i]
        error = mine - target_ref[step, i]
        gradient = error * apart(error)[1]
        slopes = jnp.zeros_like(mine)
        for k in range(1, members):
            spread = mine - everyone[step, lax.rem(me_m + k, members), i]
            slopes = slopes + spread * apart(spread)[1]
        return row_weight(i) * (gradient - slopes / (members - 1))

    def band_loss(step, i):
        states = [everyone[step, m, i] for m in range(members)]
        direct = jnp.zeros_like(states[0])
        pairs = jnp.full(direct.shape, 0.5 * members * smooth_width, F32)
        for m, state in enumerate(states):
            square, inverse = apart(state - target_ref[step, i])
            direct = direct + square * inverse
            for other in states[m + 1:]:
                square, inverse = apart(state - other)
                pairs = pairs + square * inverse
        return row_weight(i) * fold(direct - pairs / (members - 1))

    for step in range(steps):
        own = x_ref if step == 0 else fields.at[step - 1]
        if step == 0:
            front_weights()
            narrow_weights()
        act = functools.partial(bend, step)
        own_part(win, wout, own, act)
        if step < len(rounds):
            reached(step)
            if step + 1 < len(rounds):
                reach_out(step + 1)

        def advance(i, change):
            state = own[i] + change
            fields[step, i] = state
            everyone[step, me_m, i] = state
            if step < steps - 1:
                send_row(step + 1, fields.at[step], i)
            else:
                for k in peers:
                    to_member(step, k, i).start()

        convolve(win, wout, step, own, act, advance)
        if step < steps - 1:
            for i in range(rows):
                for k in peers:
                    to_member(step, k, i).start()

    back_weights()
    for step in range(steps):
        slopes_of(step)
    for r in range(steps, len(rounds)):
        reached(r)
        if r + 1 < len(rounds):
            reach_out(r + 1)
    arrive(4)
    arrive(5)
    partial = jnp.zeros((8, cols), F32)
    for step in range(steps):
        for i in reversed(range(rows)):
            landed = everyone.at[step, 0:members - 1, i]
            pltpu.make_async_copy(landed, landed, other_recv.at[step, i]).wait()
            if step < steps - 1:
                loss_grad[step, i] = loss_slopes(step, i)
            else:
                grads[step, i] = loss_slopes(step, i)
                send_row(steps, grads.at[step], i)
            if step < steps - 1 or i > 0:
                partial = partial + band_loss(step, i)

    for step in range(steps - 1, -1, -1):
        n = 2 * steps - 1 - step
        own = grads.at[step]

        def retreat(i, change):
            if step > 0:
                grads[step - 1, i] = grads[step, i] + change + loss_grad[step - 1, i]
                send_row(n + 1, grads.at[step - 1], i)
            else:
                grad_ref[mirror[i]] = grads[0, i] + change

        act = functools.partial(unbend, step)
        own_part(woutb, winb, own, act)
        if step == steps - 1:
            partial = partial + band_loss(step, 0)
            parts[me_l] = jnp.sum(partial, axis=0, keepdims=True)
            for k in range(1, bands):
                pltpu.make_async_remote_copy(
                    src_ref=parts.at[me_l], dst_ref=parts.at[me_l], send_sem=part_send.at[0], recv_sem=part_recv.at[0],
                    device_id={"lat": lax.rem(me_l + k, bands)}, device_id_type=MESH).start()
        convolve(woutb, winb, n, own, act, retreat)

    sent = parts.at[0:bands - 1]
    pltpu.make_async_copy(sent, sent, part_recv.at[0]).wait()
    total = jnp.sum(parts[...], axis=0)
    count = members * steps * rows * bands * chans * cols
    loss_ref[...] = jnp.full(loss_ref.shape, jnp.sum(total) / count, F32)
    pltpu.make_async_copy(sent, sent, part_send.at[0]).wait()
    landed = everyone.at[:, 0:members - 1]
    pltpu.make_async_copy(landed, landed, other_send.at[0]).wait()
    pltpu.make_async_copy(halo.at[:, 1], halo.at[:, 1], halo_send.at[1]).wait()

    @pl.when(has_slow)
    def _():
        pltpu.make_async_copy(halo.at[:, 0], halo.at[:, 0], halo_send.at[0]).wait()


def deliver(grad_vmem, loss_vmem, grad_hbm, loss_hbm, loss_smem, sem):
    gradient = pltpu.make_async_copy(grad_vmem, grad_hbm, sem.at[0])
    loss = pltpu.make_async_copy(loss_smem, loss_hbm, sem.at[1])
    gradient.start()
    loss_smem[0, 0] = loss_vmem[0, 0]
    loss.start()
    loss.wait()
    gradient.wait()


def on_device(members, bands, initial_states, targets, lat_weight, weight_in, weight_out, hidden_bias):
    steps, rows, chans, cols = targets.shape
    hidden = weight_in.shape[0]
    taps = 3 * chans
    depth = -(-taps // 256) * 256
    deep = 3 * hidden
    vmem = pl.BlockSpec(memory_space=pltpu.VMEM)
    dma = pltpu.SemaphoreType.DMA
    gradient, loss = pl.pallas_call(
        functools.partial(kernel, members, bands),
        out_shape=(pltpu.VMEM((rows, chans, cols), F32), pltpu.VMEM((8, cols), F32)),
        in_specs=[pl.BlockSpec(memory_space=pltpu.HBM)] * 6,
        out_specs=(vmem, vmem),
        scratch_shapes=[
            pltpu.VMEM((rows, chans, cols), F32),
            pltpu.VMEM(targets.shape, F32),
            pltpu.VMEM((1, rows), F32),
            pltpu.VMEM((3 * taps, hidden), F32),
            pltpu.VMEM((chans, 3 * deep), F32),
            pltpu.VMEM((1, hidden), F32),
            dma((6,)),
            pltpu.VMEM((2 * steps, 2, 2, chans, cols), F32),
            pltpu.VMEM((steps, members, rows, chans, cols), F32),
            pltpu.VMEM((bands, 1, cols), F32),
            pltpu.VMEM((steps, rows, chans, cols), F32),
            pltpu.VMEM((steps, rows, chans, cols), F32),
            pltpu.VMEM((3, 2 * hidden, depth), BF16),
            pltpu.VMEM((3, 2 * taps, hidden), BF16),
            pltpu.VMEM((3, 2 * taps, hidden), BF16),
            pltpu.VMEM((3, 2 * hidden, depth), BF16),
            pltpu.VMEM((depth, hidden), F32),
            pltpu.VMEM(((rows + 4) * depth, cols), BF16),
            pltpu.VMEM(((rows + 4) * depth, cols), BF16),
            pltpu.VMEM(((rows + 2) * hidden, cols), BF16),
            pltpu.VMEM(((rows + 2) * hidden, cols), BF16),
            pltpu.VMEM((rows + 2, hidden, cols), F32),
            pltpu.VMEM((steps, rows + 2, hidden, cols), F32),
            pltpu.VMEM((steps, rows + 2, hidden, cols), F32),
            pltpu.VMEM((2, taps, cols), F32),
            pltpu.VMEM((2, taps, cols), F32),
            pltpu.VMEM((steps - 1, rows, chans, cols), F32),
            pltpu.VMEM((hidden, cols), F32),
            dma((2,)), dma((2 * steps, 2)), dma((2 * steps,)),
            dma((1,)), dma((steps, rows)),
            dma((1,)), dma((1,)),
            pltpu.SemaphoreType.REGULAR((max(1, (bands - 2).bit_length()),)),
        ],
        compiler_params=pltpu.CompilerParams(collective_id=0, has_side_effects=True, vmem_limit_bytes=24 * 2**20),
    )(
        *(pltpu.with_memory_space_constraint(value, pltpu.HBM) for value in (
            initial_states.reshape(rows, chans, cols), targets, lat_weight.reshape(1, rows),
            weight_in.T, weight_out, hidden_bias.reshape(1, hidden)))
    )
    anywhere = pl.BlockSpec(memory_space=pl.ANY)
    gradient, loss = pl.pallas_call(
        deliver,
        out_shape=(jax.ShapeDtypeStruct((rows, chans, cols), F32), jax.ShapeDtypeStruct((1, 1), F32)),
        in_specs=[vmem, vmem],
        out_specs=(anywhere, anywhere),
        scratch_shapes=[pltpu.SMEM((1, 1), F32), dma((2,))],
    )(*(pltpu.with_memory_space_constraint(value, pltpu.VMEM) for value in (gradient, loss)))
    return gradient.reshape(initial_states.shape), loss.reshape(())


def solution(mesh):
    placed = (P("member", "lat", None, None), P(None, "lat", None, None), P("lat"), P(), P(), P())
    return jax.shard_map(
        functools.partial(on_device, mesh.shape["member"], mesh.shape["lat"]),
        mesh=mesh,
        in_specs=placed,
        out_specs=(P("member", "lat", None, None), P()),
        check_vma=False,
    )
```

```python
import functools

import jax
import jax.numpy as jnp
from jax import lax
from jax.experimental import pallas as pl
from jax.experimental.pallas import tpu as pltpu
from jax.sharding import PartitionSpec as P

smooth_width = 0.1
gelu_scale = 0.7978845608028654
gelu_cubic = 0.044715
MESH = pl.DeviceIdType.MESH
F32 = jnp.float32
BF16 = jnp.bfloat16


def split(value):
    high = value.astype(BF16)
    low = (value - high.astype(F32)).astype(BF16)
    return high, low


def shifted(value, tap):
    if tap == 1:
        return value
    columns = value.shape[-1]
    lane = lax.broadcasted_iota(jnp.int32, value.shape, 1)
    if tap == 0:
        return jnp.where(lane == 0, 0.0, pltpu.roll(value, 1, 1))
    return jnp.where(lane == columns - 1, 0.0, pltpu.roll(value, columns - 1, 1))


def dot(left, right):
    return jnp.dot(left, right, preferred_element_type=F32)


def kernel(
    members, bands,
    x_hbm, target_hbm, lat_hbm, w_in_hbm, w_out_hbm, bias_hbm,
    grad_ref, loss_ref,
    x_ref, target_ref, lat_ref, w_in_ref, w_out_ref, bias_ref, fetch_sem,
    halo, everyone, parts, fields, grads,
    win, winb, wout, woutb, tall, s_high, s_low, h_high, h_low, before, slope, bent, narrowed, edge, loss_grad, bias,
    halo_send, slow_recv, fast_recv, other_send, other_recv, part_send, part_recv, reach,
):
    steps, rows, chans, cols = target_ref.shape
    hidden = w_in_ref.shape[1]
    taps = 3 * chans
    depth = win.shape[2]
    me_m = lax.axis_index("member")
    me_l = lax.axis_index("lat")
    odd = lax.rem(me_l, 2)
    slow = me_l - 1 + 2 * odd
    fast = me_l + 1 - 2 * odd
    has_slow = jnp.logical_and(slow >= 0, slow < bands)
    slow = jnp.clip(slow, 0, bands - 1)

    def mirrored(n, last):
        return n + odd * (last - 2 * n)

    def fetch(n, copies):
        return [pltpu.make_async_copy(source, target, fetch_sem.at[n]) for source, target in copies]

    mirror = [mirrored(i, rows - 1) for i in range(rows)]
    fetches = [
        fetch(0, [(x_hbm.at[mirror[i]], x_ref.at[i]) for i in range(rows)]),
        fetch(1, [(w_in_hbm, w_in_ref)]),
        fetch(2, [(bias_hbm, bias_ref)]),
        fetch(3, [(w_out_hbm, w_out_ref)]),
        fetch(4, [(target_hbm.at[:, mirror[i]], target_ref.at[:, i]) for i in range(rows)]),
        fetch(5, [(lat_hbm, lat_ref)]),
    ]
    arrivals = [x_ref, w_in_ref, bias_ref, w_out_ref, target_ref, lat_ref]

    def arrive(n):
        pltpu.make_async_copy(arrivals[n], arrivals[n], fetch_sem.at[n]).wait()

    for copy in fetches[0]:
        copy.start()
    barrier = pltpu.get_barrier_semaphore()
    for k in range(1, members):
        pl.semaphore_signal(barrier, inc=1, device_id={"member": lax.rem(me_m + k, members)}, device_id_type=MESH)
    pl.semaphore_signal(barrier, inc=1, device_id={"lat": fast}, device_id_type=MESH)

    @pl.when(has_slow)
    def _():
        pl.semaphore_signal(barrier, inc=1, device_id={"lat": slow}, device_id_type=MESH)

    for copies in fetches[1:]:
        for copy in copies:
            copy.start()

    def to_slow(n, source, far):
        return pltpu.make_async_remote_copy(
            src_ref=source.at[far], dst_ref=halo.at[n, 0, far],
            send_sem=halo_send.at[0], recv_sem=slow_recv.at[n, far],
            device_id={"lat": slow}, device_id_type=MESH)

    def to_fast(n, source, far):
        return pltpu.make_async_remote_copy(
            src_ref=source.at[rows - 1 - far], dst_ref=halo.at[n, 1, far],
            send_sem=halo_send.at[1], recv_sem=fast_recv.at[n],
            device_id={"lat": fast}, device_id_type=MESH)

    def send_row(n, source, i):
        if i < 2:
            @pl.when(has_slow)
            def _():
                to_slow(n, source, i).start()

        if rows - 1 - i < 2:
            to_fast(n, source, rows - 1 - i).start()

    def peer(k):
        if members & (members - 1):
            return lax.rem(me_m + k, members)
        result, bit = 0, 1
        while bit < members:
            mine = lax.rem(me_m // bit, 2)
            result = result + bit * (1 - mine if k & bit else mine)
            bit *= 2
        return result

    peers = sorted(range(1, members), key=lambda k: -bin(k).count("1"))

    def to_member(step, k, i):
        return pltpu.make_async_remote_copy(
            src_ref=everyone.at[step, me_m, i], dst_ref=everyone.at[step, me_m, i],
            send_sem=other_send.at[0], recv_sem=other_recv.at[step, i],
            device_id={"member": peer(k)}, device_id_type=MESH)

    rounds = [1]
    while 2 * rounds[-1] < bands - 1:
        rounds.append(2 * rounds[-1])

    def reach_out(r):
        for far in (me_l - rounds[r], me_l + rounds[r]):
            @pl.when(jnp.logical_and(far >= 0, far < bands))
            def _():
                pl.semaphore_signal(
                    reach.at[r], inc=1, device_id={"lat": jnp.clip(far, 0, bands - 1)}, device_id_type=MESH)

    def reached(r):
        below = (me_l >= rounds[r]).astype(jnp.int32)
        above = (me_l + rounds[r] < bands).astype(jnp.int32)
        pl.semaphore_wait(reach.at[r], below + above)

    arrive(0)
    pl.semaphore_wait(barrier, members + has_slow.astype(jnp.int32))
    for i in reversed(range(rows)):
        send_row(0, x_ref, i)
    reach_out(0)

    def put_wide(target, a, block):
        tall[0:taps, :] = block
        high, low = split(tall[...].T)
        target[a, 0:hidden] = high
        target[a, hidden:2 * hidden] = low

    def tap_rows(a):
        return pl.ds(pl.multiple_of(mirrored(a, 2) * taps, 8), taps)

    def tap_block(a, b, size, unit):
        return pl.ds(pl.multiple_of((3 * mirrored(a, 2) + b) * size, unit), size)

    def front_weights():
        arrive(1)
        arrive(2)
        tall[taps:, :] = jnp.zeros((depth - taps, hidden), F32)
        for a in range(3):
            put_wide(win, a, w_in_ref[tap_rows(a), :])
        bias[...] = jnp.broadcast_to(bias_ref[...], (cols, hidden)).T
        for t in range(rows + 4):
            s_high[t * depth + taps:(t + 1) * depth, :] = jnp.zeros((depth - taps, cols), BF16)
            s_low[t * depth + taps:(t + 1) * depth, :] = jnp.zeros((depth - taps, cols), BF16)

    def narrow_weights():
        arrive(3)
        for a in range(3):
            for b in range(3):
                high, low = split(w_out_ref[:, tap_block(a, b, hidden, 128)])
                wout[a, b * chans:(b + 1) * chans, :] = high
                wout[a, taps + b * chans:taps + (b + 1) * chans, :] = low

    def back_weights():
        for a in range(3):
            for b in range(3):
                high, low = split(w_in_ref[tap_block(2 - a, 2 - b, chans, 8), :])
                winb[a, b * chans:(b + 1) * chans, :] = high
                winb[a, taps + b * chans:taps + (b + 1) * chans, :] = low
        for a in range(3):
            put_wide(woutb, a, jnp.concatenate(
                [w_out_ref[:, tap_block(2 - a, 2 - b, hidden, 128)] for b in range(3)], axis=0))

    def put_line(t, line):
        for b in range(3):
            high, low = split(shifted(line, b))
            at = t * depth + b * chans
            s_high[at:at + chans, :] = high
            s_low[at:at + chans, :] = low

    def joined(ref, size, lines):
        return jnp.concatenate([ref[t * size:(t + 1) * size, :] for t in lines], axis=1)

    def widen(weights, parts):
        sums = {}
        for a, lines in parts:
            high = joined(s_high, depth, lines)
            low = joined(s_low, depth, lines)
            total = jnp.concatenate([
                dot(weights[a, at:at + hidden // 2, :], high) + dot(weights[a, hidden + at:hidden + at + hidden // 2, :], high)
                + dot(weights[a, at:at + hidden // 2, :], low) for at in (0, hidden // 2)], axis=0)
            for n, t in enumerate(lines):
                line = total[:, n * cols:(n + 1) * cols]
                sums[t - a] = line if t - a not in sums else sums[t - a] + line
        return sums

    def half(weights, terms, pieces=2):
        size = weights.shape[1] // 2
        edges = [0] + [-(-size * p // (16 * pieces)) * 16 for p in range(1, pieces)] + [size]
        lines = []
        for first, last in zip(edges, edges[1:]):
            line = sum(
                dot(jnp.concatenate([weights[a, at + first:at + last, :] for at in (0, size)], axis=0), both)
                for a, both in terms)
            line = line[:, 0:cols] + line[:, cols:2 * cols]
            lines.append(line[0:last - first] + line[last - first:])
        return jnp.concatenate(lines, axis=0)

    def beside(high, low, size, t):
        return jnp.concatenate([high[t * size:(t + 1) * size, :], low[t * size:(t + 1) * size, :]], axis=1)

    def widen_line(weights, a, t, pieces=2):
        return half(weights, [(a, beside(s_high, s_low, depth, t))], pieces)

    def narrow_line(weights, *taps_of):
        return half(weights, [(a, beside(h_high, h_low, hidden, j)) for a, j in taps_of])

    def collect(total):
        return sum(shifted(total[b * chans:(b + 1) * chans], b) for b in range(3))

    def narrow(weights, parts):
        sums = {}
        for a, outs in parts:
            lines = [i + a for i in outs]
            both = dot(weights[a], joined(h_high, hidden, lines))
            total = both[0:taps] + both[taps:2 * taps] + dot(weights[a, 0:taps, :], joined(h_low, hidden, lines))
            for n, i in enumerate(outs):
                line = total[:, n * cols:(n + 1) * cols]
                sums[i] = line if i not in sums else sums[i] + line
        return sums

    def put_hidden(j, value):
        high, low = split(value)
        h_high[j * hidden:(j + 1) * hidden, :] = high
        h_low[j * hidden:(j + 1) * hidden, :] = low

    def bend(step, j, value):
        value = value + bias[...]
        inner = jnp.tanh(gelu_scale * (value + gelu_cubic * value * value * value))
        put_hidden(j, 0.5 * value * (1.0 + inner))
        slope[step, j] = value
        bent[step, j] = inner

    def slopes_of(step):
        for j in range(rows + 2):
            value, inner = slope[step, j], bent[step, j]
            slope[step, j] = 0.5 * (1.0 + inner) + 0.5 * value * (1.0 - inner * inner) * (
                gelu_scale * (1.0 + 3.0 * gelu_cubic * value * value))

    def unbend(step, j, value):
        put_hidden(j, value * slope[step, j])

    def own_part(wide, slim, own, act):
        for i in range(rows):
            put_line(i + 2, own[i])
        for j, line in widen(wide, [(a, range(2, rows + 2)) for a in range(3)]).items():
            before[j] = line

        @pl.when(jnp.logical_not(has_slow))
        def _():
            act(1, before[1])
            for i in range(2):
                edge[i] = narrow_line(slim, (1 - i, 1))

    def convolve(wide, slim, n, own, act, finish):
        pltpu.make_async_copy(halo.at[n, 1], halo.at[n, 1], fast_recv.at[n]).wait()
        for far in range(2):
            put_line(rows + 2 + far, halo[n, 1, far])
        sums = widen(wide, [(2, (rows + 2, rows + 3))])
        sums[rows + 1] = sums[rows + 1] + widen_line(wide, 1, rows + 2)
        for j in range(2, rows + 2):
            act(j, before[j] + sums[j] if j in sums else before[j])
        ready = [(a, [i for i in range(rows) if i + a >= 2]) for a in (2, 1, 0)]
        outs = narrow(slim, [part for part in ready if len(part[1]) > 1])
        for a, alone in ready:
            if len(alone) == 1:
                outs[alone[0]] = outs[alone[0]] + narrow_line(slim, (a, alone[0] + a))
        for i, line in outs.items():
            if i < 2:
                narrowed[i] = line
            else:
                finish(i, collect(line))

        @pl.when(jnp.logical_not(has_slow))
        def _():
            for i in (1, 0):
                finish(i, collect(narrowed[i] + edge[i]))

        @pl.when(has_slow)
        def _():
            to_slow(n, own, 1).wait_recv()
            put_line(0, halo[n, 0, 1])
            before[0] += widen_line(wide, 0, 0)
            to_slow(n, own, 0).wait_recv()
            put_line(1, halo[n, 0, 0])
            line1 = before[1] + widen_line(wide, 0, 1)
            line0 = before[0] + widen_line(wide, 1, 1)
            act(1, line1)
            out1 = collect(narrowed[1] + narrow_line(slim, (0, 1)))
            act(0, line0)
            finish(1, out1)
            finish(0, collect(narrowed[0] + narrow_line(slim, (1, 1), (0, 0))))

    def fold(value):
        return sum(value[8 * i:8 * i + 8] for i in range(chans // 8))

    def row_weight(i):
        return jnp.where(odd == 1, lat_ref[0:1, rows - 1 - i:rows - i], lat_ref[0:1, i:i + 1])

    def apart(spread):
        square = spread * spread + smooth_width * smooth_width
        return square, lax.rsqrt(square)

    def loss_slopes(step, i):
        mine = fields[step, i]
        error = mine - target_ref[step, i]
        gradient = error * apart(error)[1]
        slopes = jnp.zeros_like(mine)
        for k in range(1, members):
            spread = mine - everyone[step, lax.rem(me_m + k, members), i]
            slopes = slopes + spread * apart(spread)[1]
        return row_weight(i) * (gradient - slopes / (members - 1))

    def band_loss(step, i):
        states = [everyone[step, m, i] for m in range(members)]
        direct = jnp.zeros_like(states[0])
        pairs = jnp.full(direct.shape, 0.5 * members * smooth_width, F32)
        for m, state in enumerate(states):
            square, inverse = apart(state - target_ref[step, i])
            direct = direct + square * inverse
            for other in states[m + 1:]:
                square, inverse = apart(state - other)
                pairs = pairs + square * inverse
        return row_weight(i) * fold(direct - pairs / (members - 1))

    for step in range(steps):
        own = x_ref if step == 0 else fields.at[step - 1]
        if step == 0:
            front_weights()
            narrow_weights()
        act = functools.partial(bend, step)
        own_part(win, wout, own, act)
        if step < len(rounds):
            reached(step)
            if step + 1 < len(rounds):
                reach_out(step + 1)

        def advance(i, change):
            state = own[i] + change
            fields[step, i] = state
            everyone[step, me_m, i] = state
            if step < steps - 1:
                send_row(step + 1, fields.at[step], i)
            else:
                for k in peers:
                    to_member(step, k, i).start()

        convolve(win, wout, step, own, act, advance)
        if step < steps - 1:
            for i in range(rows):
                for k in peers:
                    to_member(step, k, i).start()

    back_weights()
    for step in range(steps):
        slopes_of(step)
    for r in range(steps, len(rounds)):
        reached(r)
        if r + 1 < len(rounds):
            reach_out(r + 1)
    arrive(4)
    arrive(5)
    partial = jnp.zeros((8, cols), F32)
    for step in range(steps):
        for i in reversed(range(rows)):
            landed = everyone.at[step, 0:members - 1, i]
            pltpu.make_async_copy(landed, landed, other_recv.at[step, i]).wait()
            if step < steps - 1:
                loss_grad[step, i] = loss_slopes(step, i)
            else:
                grads[step, i] = loss_slopes(step, i)
                send_row(steps, grads.at[step], i)
            if step < steps - 1 or i > 0:
                partial = partial + band_loss(step, i)

    for step in range(steps - 1, -1, -1):
        n = 2 * steps - 1 - step
        own = grads.at[step]

        def retreat(i, change):
            if step > 0:
                grads[step - 1, i] = grads[step, i] + change + loss_grad[step - 1, i]
                send_row(n + 1, grads.at[step - 1], i)
            else:
                grad_ref[mirror[i]] = grads[0, i] + change

        act = functools.partial(unbend, step)
        own_part(woutb, winb, own, act)
        if step == steps - 1:
            partial = partial + band_loss(step, 0)
            parts[me_l] = jnp.sum(partial, axis=0, keepdims=True)
            for k in range(1, bands):
                pltpu.make_async_remote_copy(
                    src_ref=parts.at[me_l], dst_ref=parts.at[me_l], send_sem=part_send.at[0], recv_sem=part_recv.at[0],
                    device_id={"lat": lax.rem(me_l + k, bands)}, device_id_type=MESH).start()
        convolve(woutb, winb, n, own, act, retreat)

    sent = parts.at[0:bands - 1]
    pltpu.make_async_copy(sent, sent, part_recv.at[0]).wait()
    total = jnp.sum(parts[...], axis=0)
    count = members * steps * rows * bands * chans * cols
    loss_ref[...] = jnp.full(loss_ref.shape, jnp.sum(total) / count, F32)
    pltpu.make_async_copy(sent, sent, part_send.at[0]).wait()
    landed = everyone.at[:, 0:members - 1]
    pltpu.make_async_copy(landed, landed, other_send.at[0]).wait()
    pltpu.make_async_copy(halo.at[:, 1], halo.at[:, 1], halo_send.at[1]).wait()

    @pl.when(has_slow)
    def _():
        pltpu.make_async_copy(halo.at[:, 0], halo.at[:, 0], halo_send.at[0]).wait()


def deliver(grad_vmem, loss_vmem, grad_hbm, loss_hbm, loss_smem, sem):
    gradient = pltpu.make_async_copy(grad_vmem, grad_hbm, sem.at[0])
    loss = pltpu.make_async_copy(loss_smem, loss_hbm, sem.at[1])
    gradient.start()
    loss_smem[0, 0] = loss_vmem[0, 0]
    loss.start()
    loss.wait()
    gradient.wait()


def on_device(members, bands, initial_states, targets, lat_weight, weight_in, weight_out, hidden_bias):
    steps, rows, chans, cols = targets.shape
    hidden = weight_in.shape[0]
    taps = 3 * chans
    depth = -(-taps // 256) * 256
    deep = 3 * hidden
    vmem = pl.BlockSpec(memory_space=pltpu.VMEM)
    dma = pltpu.SemaphoreType.DMA
    gradient, loss = pl.pallas_call(
        functools.partial(kernel, members, bands),
        out_shape=(pltpu.VMEM((rows, chans, cols), F32), pltpu.VMEM((8, cols), F32)),
        in_specs=[pl.BlockSpec(memory_space=pltpu.HBM)] * 6,
        out_specs=(vmem, vmem),
        scratch_shapes=[
            pltpu.VMEM((rows, chans, cols), F32),
            pltpu.VMEM(targets.shape, F32),
            pltpu.VMEM((1, rows), F32),
            pltpu.VMEM((3 * taps, hidden), F32),
            pltpu.VMEM((chans, 3 * deep), F32),
            pltpu.VMEM((1, hidden), F32),
            dma((6,)),
            pltpu.VMEM((2 * steps, 2, 2, chans, cols), F32),
            pltpu.VMEM((steps, members, rows, chans, cols), F32),
            pltpu.VMEM((bands, 1, cols), F32),
            pltpu.VMEM((steps, rows, chans, cols), F32),
            pltpu.VMEM((steps, rows, chans, cols), F32),
            pltpu.VMEM((3, 2 * hidden, depth), BF16),
            pltpu.VMEM((3, 2 * taps, hidden), BF16),
            pltpu.VMEM((3, 2 * taps, hidden), BF16),
            pltpu.VMEM((3, 2 * hidden, depth), BF16),
            pltpu.VMEM((depth, hidden), F32),
            pltpu.VMEM(((rows + 4) * depth, cols), BF16),
            pltpu.VMEM(((rows + 4) * depth, cols), BF16),
            pltpu.VMEM(((rows + 2) * hidden, cols), BF16),
            pltpu.VMEM(((rows + 2) * hidden, cols), BF16),
            pltpu.VMEM((rows + 2, hidden, cols), F32),
            pltpu.VMEM((steps, rows + 2, hidden, cols), F32),
            pltpu.VMEM((steps, rows + 2, hidden, cols), F32),
            pltpu.VMEM((2, taps, cols), F32),
            pltpu.VMEM((2, taps, cols), F32),
            pltpu.VMEM((steps - 1, rows, chans, cols), F32),
            pltpu.VMEM((hidden, cols), F32),
            dma((2,)), dma((2 * steps, 2)), dma((2 * steps,)),
            dma((1,)), dma((steps, rows)),
            dma((1,)), dma((1,)),
            pltpu.SemaphoreType.REGULAR((max(1, (bands - 2).bit_length()),)),
        ],
        compiler_params=pltpu.CompilerParams(collective_id=0, has_side_effects=True, vmem_limit_bytes=24 * 2**20),
    )(
        *(pltpu.with_memory_space_constraint(value, pltpu.HBM) for value in (
            initial_states.reshape(rows, chans, cols), targets, lat_weight.reshape(1, rows),
            weight_in.T, weight_out, hidden_bias.reshape(1, hidden)))
    )
    anywhere = pl.BlockSpec(memory_space=pl.ANY)
    gradient, loss = pl.pallas_call(
        deliver,
        out_shape=(jax.ShapeDtypeStruct((rows, chans, cols), F32), jax.ShapeDtypeStruct((1, 1), F32)),
        in_specs=[vmem, vmem],
        out_specs=(anywhere, anywhere),
        scratch_shapes=[pltpu.SMEM((1, 1), F32), dma((2,))],
    )(*(pltpu.with_memory_space_constraint(value, pltpu.VMEM) for value in (gradient, loss)))
    return gradient.reshape(initial_states.shape), loss.reshape(())


def solution(mesh):
    placed = (P("member", "lat", None, None), P(None, "lat", None, None), P("lat"), P(), P(), P())
    return jax.shard_map(
        functools.partial(on_device, mesh.shape["member"], mesh.shape["lat"]),
        mesh=mesh,
        in_specs=placed,
        out_specs=(P("member", "lat", None, None), P()),
        check_vma=False,
    )
```
